256 devices in a mesh: group: 2 (over z_hi), ctx: 16 (over z_lo, y), tp: 8 (over x, core).
Axes of the slice: x: 4, y: 4, z: 8 (z_hi: 2, z_lo: 4; z = z_hi * 4 + z_lo), core: 2. Of those that a mesh axis runs over, the one named last changes fastest.
Arguments:
- stretch_query: bfloat16 [2, 2048, 8192], P('group', 'ctx', 'tp'), may hold values from -8 to 8
- prefix_keyvals: bfloat16 [2, 2, 16384, 1024], P('group', None, 'ctx', 'tp'), may hold values from -6 to 6
- stretch_key_values: bfloat16 [2, 2, 2048, 1024], P('group', None, 'ctx', 'tp'), may hold values from -6 to 6
- stretch_start: int32 [2], P('group'), may hold values from 4096 to 16384
- decode_query: bfloat16 [512, 4, 8192], P(('group', 'ctx'), None, 'tp'), may hold values from -8 to 8
- draft_key_values: bfloat16 [2, 512, 4, 1024], P(None, ('group', 'ctx'), None, 'tp'), may hold values from -6 to 6
- decode_cache: bfloat16 [2, 512, 1024, 1024], P(None, ('group', 'ctx'), None, 'tp'), may hold values from -6 to 6
- cache_lengths: int32 [512], P(('group', 'ctx')), may hold values from 128 to 1024, as said below
- page_rows: int32 [32], replicated, may hold values from 0 to 511, as said below
Outputs:
- prefill_out: bfloat16 [2, 2048, 8192], P('group', 'ctx', 'tp')
- decode_out: bfloat16 [512, 4, 8192], P(('group', 'ctx'), None, 'tp')
The draws below stay inside these ranges and needn't reach their ends.
Inputs may be any that keep to these rules, and one draw needn't show every extreme that they name: `cache_lengths`: one row has length 1024. `page_rows`: page n = g * 16 + c names one of the rows m * 16 to m * 16 + 15, where m = (n + 1) mod 32 if n mod 4 = 1, m = g * 16 + (c + 16 / 2) mod 16 if n mod 4 = 3, and m = (n + 16) mod 32 for even n; no row is named twice.
All inputs are finite; a program needn't handle non-finite values.
Results may differ from the reference program's by a relative error of at most 0.0049.
Values may be sent and summed in bfloat16 or wider, within the bound.
No kernel may reach another device: no remote copies, remote signals or barrier semaphores. Data moves between devices by JAX's collectives and lax.ppermute only.
A program may use at most 128 MiB of HBM per device.

```python
import math
import jax
import jax.numpy as jnp
from jax import lax

QUERY_HEADS = 64
KEY_VALUE_HEADS = 8
HEAD_SIZE = 128
STRETCH_DEV = 128
ROWS_DEV = 16
ROW_CACHE_LIMIT = 1024
DRAFT_TOKENS = 4
QUERY_GROUP = 8
PREFILL_COUNT = 2
STRETCH_LENGTH = 2048
PREFIX_LENGTH = 16384
DECODE_ROWS = 512
PAGES = 32
N_CTX = 16


def draw_stretch_query(key, part):
    local = jax.random.fold_in(key, 11)
    values = jnp.clip(2.5 * jax.random.normal(local, (PREFILL_COUNT, STRETCH_LENGTH, QUERY_HEADS * HEAD_SIZE), jnp.float32), -8.0, 8.0)
    return values.astype(jnp.bfloat16)


def draw_prefix_keyvals(key, part):
    local = jax.random.fold_in(key, 21)
    array_shape = (PREFILL_COUNT, 2, PREFIX_LENGTH, KEY_VALUE_HEADS * HEAD_SIZE)
    values = jnp.clip(jax.random.normal(local, array_shape, jnp.float32), -6.0, 6.0)
    return values.astype(jnp.bfloat16)


def draw_decode_query(key, part):
    local = jax.random.fold_in(key, 31)
    array_shape = (DECODE_ROWS, DRAFT_TOKENS, QUERY_HEADS * HEAD_SIZE)
    values = jnp.clip(2.5 * jax.random.normal(local, array_shape, jnp.float32), -8.0, 8.0)
    return values.astype(jnp.bfloat16)


def draw_decode_cache(key, part):
    local = jax.random.fold_in(key, 41)
    array_shape = (2, DECODE_ROWS, ROW_CACHE_LIMIT, KEY_VALUE_HEADS * HEAD_SIZE)
    values = jnp.clip(jax.random.normal(local, array_shape, jnp.float32), -6.0, 6.0)
    return values.astype(jnp.bfloat16)


def draw_cache_lengths(key, part):
    blocks = DECODE_ROWS // ROWS_DEV
    levels = (ROW_CACHE_LIMIT // STRETCH_DEV).bit_length() - 1
    power = jax.random.randint(jax.random.fold_in(key, 51), (blocks, 1), 0, levels + 1)
    ceiling = STRETCH_DEV * 2 ** power
    spread = jax.random.randint(jax.random.fold_in(key, 52), (blocks, ROWS_DEV), 0, ceiling - STRETCH_DEV + 1)
    lengths = (STRETCH_DEV + spread).reshape(DECODE_ROWS)
    longest = jax.random.randint(jax.random.fold_in(key, 53), (), 0, DECODE_ROWS)
    lengths = jnp.where(jnp.arange(DECODE_ROWS) == longest, ROW_CACHE_LIMIT, lengths)
    return lengths.astype(jnp.int32)


def draw_page_rows(key, part):
    page_ids = jnp.arange(PAGES, dtype=jnp.int32)
    kind = page_ids % 4
    odd_page = page_ids % 2 == 1
    position = page_ids % N_CTX
    half_away = page_ids - position + (position + N_CTX // 2) % N_CTX
    target_block = jnp.where(kind == 1, page_ids + 1, jnp.where(kind == 3, half_away, page_ids + PAGES // 2)) % PAGES
    first_row = jax.random.randint(jax.random.fold_in(key, 61), (PAGES,), 0, ROWS_DEV)
    second_row = (first_row + 1 + jax.random.randint(jax.random.fold_in(key, 62), (PAGES,), 0, ROWS_DEV - 1)) % ROWS_DEV
    within = jnp.where(odd_page, first_row[target_block], second_row[target_block])
    return (target_block * ROWS_DEV + within).astype(jnp.int32)


def level_of(stream_key, shape, pieces, low, largest):
    loudness = 1.0
    for axis_at, shards_of in pieces:
        steps = jax.random.uniform(jax.random.fold_in(jax.random.fold_in(stream_key, 6), axis_at), (shards_of,), jnp.float32, low / len(pieces), largest / len(pieces))
        loudness = loudness * jnp.repeat(jnp.exp(steps), shape[axis_at] // shards_of).reshape((-1,) + (1,) * (len(shape) - 1 - axis_at))
    return loudness


def gaussian(own_key, dims, scale, most, split=(), kind=jnp.bfloat16):
    gain = level_of(own_key, dims, split, -0.22, 0.18) if split else 1.0
    drawn = jax.random.normal(own_key, dims, jnp.float32) * scale * gain
    return jnp.minimum(jnp.maximum(drawn, -most), most).astype(kind)


def setup_inputs(seed: int = 0) -> dict:
    streams_of = jax.random.split(jax.random.key(seed), 10)
    stretch_query = draw_stretch_query(jax.random.fold_in(streams_of[9], 71), 0)
    prefix_keyvals = draw_prefix_keyvals(jax.random.fold_in(streams_of[9], 71), 0)
    stretch_key_values = gaussian(streams_of[2], (PREFILL_COUNT, 2, STRETCH_LENGTH, KEY_VALUE_HEADS * HEAD_SIZE), 1.0, 6.0, ((0, 2), (2, 16), (3, 8)))
    stretch_start = jax.random.randint(streams_of[3], (PREFILL_COUNT,), PREFIX_LENGTH // 4, PREFIX_LENGTH + 1).astype(jnp.int32)
    decode_query = draw_decode_query(jax.random.fold_in(streams_of[9], 71), 0)
    draft_key_values = gaussian(streams_of[5], (2, DECODE_ROWS, DRAFT_TOKENS, KEY_VALUE_HEADS * HEAD_SIZE), 1.0, 6.0, ((1, 32), (3, 8)))
    decode_cache = draw_decode_cache(jax.random.fold_in(streams_of[9], 71), 0)
    cache_lengths = draw_cache_lengths(jax.random.fold_in(streams_of[9], 71), 0)
    page_rows = draw_page_rows(jax.random.fold_in(streams_of[9], 71), 0)
    return dict(stretch_query=stretch_query, prefix_keyvals=prefix_keyvals, stretch_key_values=stretch_key_values, stretch_start=stretch_start, decode_query=decode_query, draft_key_values=draft_key_values, decode_cache=decode_cache, cache_lengths=cache_lengths, page_rows=page_rows)


def attend_rows(queries, rows_of_keys, rows_of_values, allowed):
    scores = jnp.dot(queries, rows_of_keys.T, preferred_element_type=jnp.float32) * (1.0 / math.sqrt(HEAD_SIZE))
    masked = jnp.where(allowed, scores, -jnp.inf)
    highest = lax.optimization_barrier(jnp.max(masked, axis=-1, keepdims=True))
    weights = jnp.exp(masked - highest)
    totals = lax.optimization_barrier(jnp.sum(weights, axis=-1, keepdims=True))
    summed = jnp.dot(weights.astype(jnp.bfloat16), rows_of_values, preferred_element_type=jnp.float32)
    return (summed / totals).astype(jnp.bfloat16)

def prefill_request(query, prefix_length, stretch_length, limit):
    total_length = PREFIX_LENGTH + STRETCH_LENGTH
    heads_q = query.reshape(STRETCH_LENGTH, QUERY_HEADS, HEAD_SIZE).transpose(1, 0, 2)
    joined_keys = jnp.concatenate([prefix_length[0], stretch_length[0]], axis=0).reshape(total_length, KEY_VALUE_HEADS, HEAD_SIZE).transpose(1, 0, 2)
    joined_values = jnp.concatenate([prefix_length[1], stretch_length[1]], axis=0).reshape(total_length, KEY_VALUE_HEADS, HEAD_SIZE).transpose(1, 0, 2)
    key_pos = jnp.arange(total_length, dtype=jnp.int32)
    query_pos = jnp.arange(STRETCH_LENGTH, dtype=jnp.int32)
    allowed = jnp.where(key_pos[None, :] < PREFIX_LENGTH, key_pos[None, :] < limit, (key_pos - PREFIX_LENGTH)[None, :] <= query_pos[:, None])

    def one_head(head_index):
        kv_index = head_index // QUERY_GROUP
        return attend_rows(heads_q[head_index], joined_keys[kv_index], joined_values[kv_index], allowed)
    result = lax.map(one_head, jnp.arange(QUERY_HEADS, dtype=jnp.int32))
    return result.transpose(1, 0, 2).reshape(STRETCH_LENGTH, QUERY_HEADS * HEAD_SIZE)

def reference(stretch_query, prefix_keyvals, stretch_key_values, stretch_start, decode_query, draft_key_values, decode_cache, cache_lengths, page_rows):
    results = []
    for request in range(PREFILL_COUNT):
        results.append(prefill_request(stretch_query[request], prefix_keyvals[request], stretch_key_values[request], stretch_start[request]))
    prefill_out = jnp.stack(results)
    column_count = KEY_VALUE_HEADS * HEAD_SIZE
    pages = stretch_key_values.reshape(PREFILL_COUNT, 2, N_CTX, STRETCH_DEV, column_count).transpose(0, 2, 1, 3, 4).reshape(PAGES, 2, STRETCH_DEV, column_count)
    token_span = ROW_CACHE_LIMIT + DRAFT_TOKENS
    key_pos = jnp.arange(token_span, dtype=jnp.int32)
    step_pos = jnp.arange(DRAFT_TOKENS, dtype=jnp.int32)

    def one_row(row_index):
        matches = page_rows == row_index
        has_page = jnp.any(matches)
        page_block = jnp.einsum('p,pcsd->csd', matches.astype(jnp.float32), pages.astype(jnp.float32)).astype(jnp.bfloat16)
        row_cache = decode_cache[:, row_index]
        head_part = jnp.where(has_page, page_block, row_cache[:, :STRETCH_DEV])
        fresh = draft_key_values[:, row_index]
        rows_of_keys = jnp.concatenate([head_part[0], row_cache[0, STRETCH_DEV:], fresh[0]], axis=0)
        rows_of_values = jnp.concatenate([head_part[1], row_cache[1, STRETCH_DEV:], fresh[1]], axis=0)
        heads_of_keys = jnp.repeat(rows_of_keys.reshape(token_span, KEY_VALUE_HEADS, HEAD_SIZE).transpose(1, 0, 2), QUERY_GROUP, axis=0)
        heads_of_values = jnp.repeat(rows_of_values.reshape(token_span, KEY_VALUE_HEADS, HEAD_SIZE).transpose(1, 0, 2), QUERY_GROUP, axis=0)
        allowed = jnp.where(key_pos[None, :] < ROW_CACHE_LIMIT, key_pos[None, :] < cache_lengths[row_index], (key_pos - ROW_CACHE_LIMIT)[None, :] <= step_pos[:, None])
        heads_q = decode_query[row_index].reshape(DRAFT_TOKENS, QUERY_HEADS, HEAD_SIZE).transpose(1, 0, 2)
        result = jax.vmap(attend_rows, in_axes=(0, 0, 0, None))(heads_q, heads_of_keys, heads_of_values, allowed)
        return result.transpose(1, 0, 2).reshape(DRAFT_TOKENS, QUERY_HEADS * HEAD_SIZE)
    decode_out = lax.map(one_row, jnp.arange(DECODE_ROWS, dtype=jnp.int32))
    return (prefill_out, decode_out)
```

```python
import functools
import math

import jax
import jax.numpy as jnp
from jax import lax
from jax.experimental import pallas as pl
from jax.experimental.pallas import tpu as pltpu
from jax.sharding import PartitionSpec as P

HEAD = 128
GROUP = 8
ROWS = 1024
PREFIX = 1024
PAGE = 128
KEYS = PREFIX + PAGE
NORM_AT = 2 * KEYS
MSG_ROWS = NORM_AT + 16
STATE_ROWS = 144
HALF = 512
SCALE2 = math.log2(math.e) / math.sqrt(HEAD)
EMPTY = -1e30
SAFE = 75.0 * 75.0 * HEAD
Q_OFFSETS = ((0, 0), (2, 0), (0, 3), (2, 3))
K_OFFSETS = ((0, 0), (1, 0), (0, 1), (1, 1))


def xor_pairs(dz, dy):
    return [(z * 4 + y, (z ^ dz) * 4 + (y ^ dy)) for z in range(4) for y in range(4)]


def squares_max(rows):
    ones = jnp.ones((HEAD, HEAD), jnp.bfloat16)
    return jnp.max(jnp.dot(rows * rows, ones, preferred_element_type=jnp.float32))


def prepare_kernel(prefix_ref, stretch_ref, msg_ref):
    msg_ref[:PREFIX] = prefix_ref[0, 0]
    msg_ref[PREFIX:KEYS] = stretch_ref[0, 0]
    for j in range(PREFIX // PAGE):
        msg_ref[KEYS + j * PAGE : KEYS + (j + 1) * PAGE] = prefix_ref[0, 1, j * PAGE : (j + 1) * PAGE].T
    msg_ref[KEYS + PREFIX : NORM_AT] = stretch_ref[0, 1].T
    largest = squares_max(msg_ref[:KEYS]) * 1.02
    msg_ref[NORM_AT:] = jnp.full((16, HEAD), largest, jnp.float32).astype(jnp.bfloat16)


def prepare(prefix, stretch):
    return pl.pallas_call(
        prepare_kernel,
        out_shape=jax.ShapeDtypeStruct((MSG_ROWS, HEAD), jnp.bfloat16),
        compiler_params=pltpu.CompilerParams(vmem_limit_bytes=16 << 20),
        name="prepare",
    )(prefix, stretch)


def effective(state):
    total = jnp.sum(state[128:136], axis=0, keepdims=True)
    return total, jnp.where(total > 0.0, state[136:137], EMPTY)


def combine(first, second):
    total_a, max_a = effective(first)
    total_b, max_b = effective(second)
    top = jnp.maximum(max_a, max_b)
    factor_a, factor_b = jnp.exp2(max_a - top), jnp.exp2(max_b - top)
    summed = first[:128] * factor_a + second[:128] * factor_b
    return summed, total_a * factor_a + total_b * factor_b, top


def fold_kernel(meta, *refs, n_q, n_k, q_at, k_at, prior_at, message):
    q_hbm, refs = refs[:n_q], refs[n_q:]
    k_hbm, refs = refs[:n_k], refs[n_k:]
    if prior_at is not None:
        prior_hbm, refs = refs[0], refs[1:]
    out_ref, qs, ks, vt, norms, state, *rest = refs
    sems = rest[-1]
    copies = []

    def copy(source, target):
        made = pltpu.make_async_copy(source, target, sems.at[len(copies)])
        made.start()
        copies.append(made)

    for i in range(n_q):
        for h in range(GROUP):
            columns = slice(h * HEAD, (h + 1) * HEAD)
            copy(q_hbm[i].at[:, columns], qs.at[i, columns, :])
    for i in range(n_k):
        copy(k_hbm[i].at[pl.ds(0, KEYS)], ks.at[i])
        copy(k_hbm[i].at[pl.ds(NORM_AT, 16)], norms.at[i])
        for j in range(KEYS // PAGE):
            columns = slice(j * PAGE, (j + 1) * PAGE)
            copy(k_hbm[i].at[pl.ds(KEYS + j * PAGE, PAGE)], vt.at[i, :, columns])
    if prior_at is not None:
        prior = rest[0]
        for i in range(n_q):
            copy(prior_hbm.at[prior_at + i], prior.at[i])
    for made in copies:
        made.wait()

    largest_q = functools.reduce(jnp.maximum, [squares_max(qs[i]) for i in range(n_q)]) * 1.02
    largest_k = jnp.max(norms[...].astype(jnp.float32)) * 1.01
    safe = largest_q * largest_k <= SAFE
    limit = meta[0]

    def parts(t, block):
        qi, ki = t // n_k, t % n_k
        q_ctx, k_ctx = meta[4 + q_at + qi], meta[8 + k_at + ki]
        valid = limit - k_ctx * PREFIX

        def prefix_mask(at, rows):
            return lambda: lax.broadcasted_iota(jnp.int32, (rows, ROWS), 0) < valid - at

        def causal_mask():
            token = lax.broadcasted_iota(jnp.int32, (PAGE, ROWS), 1) & (PAGE - 1)
            return k_ctx * PAGE + lax.broadcasted_iota(jnp.int32, (PAGE, ROWS), 0) <= q_ctx * PAGE + token

        @pl.when(valid >= PREFIX)
        def _():
            for at in range(0, PREFIX, HALF):
                block(qi, ki, at, HALF, None)

        @pl.when((valid > 0) & (valid < PREFIX))
        def _():
            for at in range(0, PREFIX, HALF):
                pl.when(valid > at)(functools.partial(block, qi, ki, at, HALF, prefix_mask(at, HALF)))

        @pl.when(k_ctx <= q_ctx)
        def _():
            block(qi, ki, PREFIX, PAGE, causal_mask)

    def scores_of(qi, ki, at, rows):
        keys = ks[ki, at : at + rows, :]
        return lax.dot_general(keys, qs[qi], (((1,), (1,)), ((), ())), preferred_element_type=jnp.float32) * SCALE2

    def fast_block(qi, ki, at, rows, mask):
        weights = jnp.exp2(scores_of(qi, ki, at, rows))
        if mask is not None:
            weights = jnp.where(mask(), weights, 0.0)
        state[qi, 128:136] += jnp.sum(weights.reshape(rows // 8, 8, ROWS), axis=0)
        state[qi, :128] += jnp.dot(
            vt[ki, :, at : at + rows], weights.astype(jnp.bfloat16), preferred_element_type=jnp.float32
        )

    def general_block(qi, ki, at, rows, mask):
        scores = scores_of(qi, ki, at, rows)
        if mask is not None:
            scores = jnp.where(mask(), scores, EMPTY)
        before = state[qi, 136:137]
        top = jnp.maximum(before, jnp.max(scores, axis=0, keepdims=True))
        factor = jnp.exp2(before - top)
        weights = jnp.exp2(scores - top)
        state[qi, 136:144] = jnp.broadcast_to(top, (8, ROWS))
        state[qi, 128:136] = state[qi, 128:136] * factor + jnp.sum(weights.reshape(rows // 8, 8, ROWS), axis=0)
        state[qi, :128] = state[qi, :128] * factor + jnp.dot(
            vt[ki, :, at : at + rows], weights.astype(jnp.bfloat16), preferred_element_type=jnp.float32
        )

    state[:, :136] = jnp.zeros((n_q, 136, ROWS), jnp.float32)

    @pl.when(safe)
    def _():
        state[:, 136:] = jnp.zeros((n_q, 8, ROWS), jnp.float32)
        lax.fori_loop(0, n_q * n_k, lambda t, c: (parts(t, fast_block), c)[1], 0)

    @pl.when(jnp.logical_not(safe))
    def _():
        state[:, 136:] = jnp.full((n_q, 8, ROWS), EMPTY, jnp.float32)
        lax.fori_loop(0, n_q * n_k, lambda t, c: (parts(t, general_block), c)[1], 0)

    for i in range(n_q):
        if prior_at is not None:
            summed, total, top = combine(prior[i], state[i])
        elif message:
            total, top = effective(state[i])
            summed = state[i, :128]
        if message:
            sent = jnp.where(top > EMPTY, 4.0 * jnp.ceil(top * 0.25), EMPTY)
            factor = jnp.exp2(top - sent)
            total = total * factor
            high = total.astype(jnp.bfloat16).astype(jnp.float32)
            row = lax.broadcasted_iota(jnp.int32, (16, ROWS), 0)
            tail = jnp.where(row == 0, high, jnp.where(row == 1, total - high, jnp.where(row == 2, sent, 0.0)))
            out_ref[i, :128] = (summed * factor).astype(jnp.bfloat16)
            out_ref[i, 128:] = tail.astype(jnp.bfloat16)
        elif prior_at is not None:
            row = lax.broadcasted_iota(jnp.int32, (16, ROWS), 0)
            out_ref[i, :128] = summed
            out_ref[i, 128:] = jnp.where(row == 0, total, jnp.where(row < 8, 0.0, top))
        else:
            out_ref[i] = state[i]


def fold(meta, queries, keys, q_at, k_at, prior=None, prior_at=None, message=False, name="fold"):
    n_q, n_k = len(queries), len(keys)
    anywhere = pl.BlockSpec(memory_space=pl.ANY)
    inputs = list(queries) + list(keys) + ([prior] if prior is not None else [])
    scratch = [
        pltpu.VMEM((n_q, ROWS, HEAD), jnp.bfloat16),
        pltpu.VMEM((n_k, KEYS, HEAD), jnp.bfloat16),
        pltpu.VMEM((n_k, HEAD, KEYS), jnp.bfloat16),
        pltpu.VMEM((n_k, 16, HEAD), jnp.bfloat16),
        pltpu.VMEM((n_q, STATE_ROWS, ROWS), jnp.float32),
    ]
    n_copies = 8 * n_q + 11 * n_k
    if prior is not None:
        scratch.append(pltpu.VMEM((n_q, STATE_ROWS, ROWS), jnp.float32))
        n_copies += n_q
    scratch.append(pltpu.SemaphoreType.DMA((n_copies,)))
    work = 4 * n_q * n_k * ROWS * KEYS * HEAD
    return pl.pallas_call(
        functools.partial(
            fold_kernel, n_q=n_q, n_k=n_k, q_at=q_at, k_at=k_at, prior_at=prior_at, message=message
        ),
        out_shape=jax.ShapeDtypeStruct((n_q, STATE_ROWS, ROWS), jnp.bfloat16 if message else jnp.float32),
        in_specs=[pl.BlockSpec(memory_space=pltpu.SMEM)] + [anywhere] * len(inputs),
        scratch_shapes=scratch,
        compiler_params=pltpu.CompilerParams(vmem_limit_bytes=48 << 20),
        cost_estimate=pl.CostEstimate(flops=2 * work, transcendentals=n_q * n_k * ROWS * KEYS, bytes_accessed=n_k * 600000),
        name=name,
    )(meta, *inputs)


def merge_kernel(own_ref, *refs):
    message_refs, out_ref = refs[:-1], refs[-1]
    total, top = effective(own_ref[0])
    tops, totals, sums = [top], [total], [own_ref[0, :128]]
    for ref in message_refs:
        tail = ref[0, 128:].astype(jnp.float32)
        tops.append(tail[2:3])
        totals.append(tail[0:1] + tail[1:2])
        sums.append(ref[0, :128].astype(jnp.float32))
    top = functools.reduce(jnp.maximum, tops)
    factors = [jnp.exp2(t - top) for t in tops]
    total = functools.reduce(jnp.add, [t * f for t, f in zip(totals, factors)])
    inverse = 1.0 / total
    attended = functools.reduce(jnp.add, [s * (f * inverse) for s, f in zip(sums, factors)])
    for h in range(GROUP):
        columns = slice(h * HEAD, (h + 1) * HEAD)
        out_ref[0, :, columns] = attended[:, columns].T.astype(jnp.bfloat16)


def merge(own, messages):
    return pl.pallas_call(
        merge_kernel,
        out_shape=jax.ShapeDtypeStruct((1, PAGE, ROWS), jnp.bfloat16),
        compiler_params=pltpu.CompilerParams(vmem_limit_bytes=16 << 20),
        name="merge",
    )(own, *messages)


def decode_kernel(meta, lengths, q_ref, cache_ref, draft_ref, page_a, page_b, out_ref, *, steps):
    r = pl.program_id(0)
    row_a, row_b, length = meta[1], meta[2], lengths[r]
    queries = q_ref[0]
    rows = queries.shape[0]
    limit = cache_ref.shape[2]

    def with_page(kind):
        block = cache_ref[kind, 0]
        first = jnp.where(r == row_a, page_a[0, kind], jnp.where(r == row_b, page_b[0, kind], block[:PAGE]))
        return jnp.concatenate([first, block[PAGE:]], axis=0)

    def product(keys):
        return lax.dot_general(
            queries, keys, (((1,), (1,)), ((), ())), preferred_element_type=jnp.float32
        ) * SCALE2

    scores = product(with_page(0))
    scores = jnp.where(lax.broadcasted_iota(jnp.int32, (rows, limit), 1) < length, scores, -jnp.inf)
    draft = product(draft_ref[0, 0])
    step = lax.broadcasted_iota(jnp.int32, (rows, steps), 0) // GROUP
    draft = jnp.where(lax.broadcasted_iota(jnp.int32, (rows, steps), 1) <= step, draft, -jnp.inf)
    top = jnp.maximum(jnp.max(scores, axis=1, keepdims=True), jnp.max(draft, axis=1, keepdims=True))
    weights, draft_weights = jnp.exp2(scores - top), jnp.exp2(draft - top)
    total = jnp.sum(weights, axis=1, keepdims=True) + jnp.sum(draft_weights, axis=1, keepdims=True)
    summed = jnp.dot(weights.astype(jnp.bfloat16), with_page(1), preferred_element_type=jnp.float32)
    summed += jnp.dot(draft_weights.astype(jnp.bfloat16), draft_ref[1, 0], preferred_element_type=jnp.float32)
    out_ref[0] = (summed / total).astype(jnp.bfloat16)


def decode(meta, lengths, queries, cache, draft, page_a, page_b):
    row_count, rows, _ = queries.shape
    steps = draft.shape[2]
    limit = cache.shape[2]
    smem = pl.BlockSpec(memory_space=pltpu.SMEM)
    page_spec = pl.BlockSpec((1, 2, PAGE, HEAD), lambda r: (0, 0, 0, 0))
    return pl.pallas_call(
        functools.partial(decode_kernel, steps=steps),
        grid=(row_count,),
        out_shape=jax.ShapeDtypeStruct(queries.shape, jnp.bfloat16),
        in_specs=[
            smem,
            smem,
            pl.BlockSpec((1, rows, HEAD), lambda r: (r, 0, 0)),
            pl.BlockSpec((2, 1, limit, HEAD), lambda r: (0, r, 0, 0)),
            pl.BlockSpec((2, 1, steps, HEAD), lambda r: (0, r, 0, 0)),
            page_spec,
            page_spec,
        ],
        out_specs=pl.BlockSpec((1, rows, HEAD), lambda r: (r, 0, 0)),
        compiler_params=pltpu.CompilerParams(vmem_limit_bytes=16 << 20),
        cost_estimate=pl.CostEstimate(
            flops=32 * row_count * rows * limit * HEAD, transcendentals=row_count * rows * limit, bytes_accessed=8 << 20
        ),
        name="decode",
    )(meta, lengths, queries, cache, draft, page_a, page_b)


def page_targets():
    first, second = [], []
    for n in range(32):
        g, c = n // 16, n % 16
        if n % 4 == 1:
            second.append((n, (n + 1) % 32))
        elif n % 4 == 3:
            first.append((n, g * 16 + (c + 8) % 16))
        else:
            first.append((n, (n + 16) % 32))
    return first, second


def on_device(
    stretch_query,
    prefix_keyvals,
    stretch_key_values,
    stretch_start,
    decode_query,
    draft_key_values,
    decode_cache,
    cache_lengths,
    page_rows,
):
    ctx = lax.axis_index("ctx")
    z, y = ctx // 4, ctx % 4
    block = lax.axis_index(("group", "ctx"))
    row_count, steps, _ = decode_query.shape

    kind = block % 4
    source_a = jnp.where(kind == 3, block - block % 16 + (block + 8) % 16, (block + 16) % 32)
    source_b = jnp.maximum(block - 1, 0)
    row_a = jnp.where(kind == 1, -1, page_rows[source_a] - block * row_count)
    row_b = jnp.where(kind == 2, page_rows[source_b] - block * row_count, -1)
    zero = jnp.zeros((), jnp.int32)
    meta = jnp.stack(
        [stretch_start[0], row_a, row_b, zero]
        + [(z ^ dz) * 4 + (y ^ dy) for dz, dy in Q_OFFSETS]
        + [(z ^ dz) * 4 + (y ^ dy) for dz, dy in K_OFFSETS]
    ).astype(jnp.int32)

    query = stretch_query[0]
    send = lambda x, dz, dy: lax.ppermute(x, "ctx", xor_pairs(dz, dy))
    first, second = page_targets()
    page_a = lax.ppermute(stretch_key_values, ("group", "ctx"), first)
    page_b = lax.ppermute(stretch_key_values, ("group", "ctx"), second)
    query_z = send(query, 2, 0)
    query_y = send(query, 0, 3)
    own = prepare(prefix_keyvals, stretch_key_values)
    keys_z = send(own, 1, 0)
    keys_y = send(own, 0, 1)
    query_d = send(query_z, 0, 3)
    keys_d = send(keys_z, 0, 1)

    decode_rows = decode_query.reshape(row_count, steps * GROUP, HEAD)
    decoded = decode(meta, cache_lengths, decode_rows, decode_cache, draft_key_values, page_a, page_b)
    decode_out = decoded.reshape(decode_query.shape)

    near = fold(meta, [query, query_z, query_y], [own, keys_z, keys_y], 0, 0, name="fold_near")
    message_d = fold(meta, [query_d], [own, keys_z, keys_y, keys_d], 3, 0, message=True, name="fold_far")
    messages = fold(meta, [query_z, query_y], [keys_d], 1, 3, prior=near, prior_at=1, message=True, name="fold_two")
    from_d = send(message_d, 2, 3)
    from_z = send(messages[0:1], 2, 0)
    from_y = send(messages[1:2], 0, 3)
    final = fold(meta, [query], [keys_d], 0, 3, prior=near, prior_at=0, name="fold_own")
    prefill_out = merge(final, [from_d, from_z, from_y])
    return (prefill_out, decode_out)


def solution(mesh):
    return jax.shard_map(
        on_device,
        mesh=mesh,
        in_specs=(
            P("group", "ctx", "tp"),
            P("group", None, "ctx", "tp"),
            P("group", None, "ctx", "tp"),
            P("group"),
            P(("group", "ctx"), None, "tp"),
            P(None, ("group", "ctx"), None, "tp"),
            P(None, ("group", "ctx"), None, "tp"),
            P(("group", "ctx")),
            P(),
        ),
        out_specs=(P("group", "ctx", "tp"), P(("group", "ctx"), None, "tp")),
        check_vma=False,
    )
```

```python
import functools
import math

import jax
import jax.numpy as jnp
from jax import lax
from jax.experimental import pallas as pl
from jax.experimental.pallas import tpu as pltpu
from jax.sharding import PartitionSpec as P

HEAD = 128
GROUP = 8
ROWS = 1024
PREFIX = 1024
PAGE = 128
KEYS = PREFIX + PAGE
HALF = 512
NORM_AT = 2 * HALF
STRETCH_AT = NORM_AT + 16
FIRST_ROWS = STRETCH_AT + 2 * PAGE
SECOND_ROWS = STRETCH_AT
QUERY_ROWS = ROWS + 16
STATE_ROWS = 144
SCALE2 = math.log2(math.e) / math.sqrt(HEAD)
EMPTY = -1e30
SAFE = 75.0 * 75.0 * HEAD
Q_OFFSETS = ((0, 0), (1, 3), (1, 0), (0, 3))
K_OFFSETS = ((0, 0), (0, 1), (2, 0), (2, 1))


def xor_pairs(dz, dy):
    return [(z * 4 + y, (z ^ dz) * 4 + (y ^ dy)) for z in range(4) for y in range(4)]


def block_of(ctx, dz, dy):
    z, y = ctx // 4, ctx % 4
    flip = {0: lambda v: v, 1: lambda v: v + 1 - 2 * (v % 2), 2: lambda v: (v + 2) % 4, 3: lambda v: 3 - v}
    return flip[dz](z) * 4 + flip[dy](y)


def squares_max(rows):
    ones = jnp.ones((HEAD, HEAD), jnp.bfloat16)
    return jnp.max(jnp.dot(rows * rows, ones, preferred_element_type=jnp.float32))


def norm_rows(rows):
    return jnp.full((16, HEAD), squares_max(rows) * 1.04, jnp.float32).astype(jnp.bfloat16)


def prepare_kernel(query_hbm, prefix_hbm, stretch_hbm, query_msg, whole, first, second, keys, values, sems):
    copies = [
        (query_hbm.at[0, :, h * HEAD : (h + 1) * HEAD], query_msg.at[h * HEAD : (h + 1) * HEAD]) for h in range(GROUP)
    ]
    copies += [
        (prefix_hbm.at[0, 0], keys.at[:PREFIX]),
        (stretch_hbm.at[0, 0], keys.at[PREFIX:]),
        (prefix_hbm.at[0, 1], values.at[:PREFIX]),
        (stretch_hbm.at[0, 1], values.at[PREFIX:]),
    ]
    copies = [pltpu.make_async_copy(a, b, sems.at[i]) for i, (a, b) in enumerate(copies)]
    for made in copies:
        made.start()
    for made in copies[GROUP:]:
        made.wait()
    norms = norm_rows(keys[...])
    for at, part, base in ((0, first, 0), (HALF, second, FIRST_ROWS)):
        pieces = [(0, keys[at : at + HALF]), (NORM_AT, norms)]
        pieces += [(HALF + j, values[at + j : at + j + PAGE].T) for j in range(0, HALF, PAGE)]
        if base == 0:
            pieces += [(STRETCH_AT, keys[PREFIX:]), (STRETCH_AT + PAGE, values[PREFIX:].T)]
        for row, piece in pieces:
            part[row : row + piece.shape[0]] = piece
            whole[base + row : base + row + piece.shape[0]] = piece
    for made in copies[:GROUP]:
        made.wait()
    query_msg[ROWS:] = norm_rows(query_msg[:ROWS])


def prepare(query, prefix, stretch):
    in_hbm = [pltpu.with_memory_space_constraint(x, pltpu.HBM) for x in (query, prefix, stretch)]
    return pl.pallas_call(
        prepare_kernel,
        out_shape=[
            jax.ShapeDtypeStruct((rows, HEAD), jnp.bfloat16)
            for rows in (QUERY_ROWS, FIRST_ROWS + SECOND_ROWS, FIRST_ROWS, SECOND_ROWS)
        ],
        in_specs=[pl.BlockSpec(memory_space=pl.ANY)] * 3,
        scratch_shapes=[
            pltpu.VMEM((KEYS, HEAD), jnp.bfloat16),
            pltpu.VMEM((KEYS, HEAD), jnp.bfloat16),
            pltpu.SemaphoreType.DMA((GROUP + 4,)),
        ],
        compiler_params=pltpu.CompilerParams(vmem_limit_bytes=16 << 20),
        name="prepare",
    )(*in_hbm)


def effective(state):
    total = jnp.sum(state[128:136], axis=0, keepdims=True)
    return total, jnp.where(total > 0.0, state[136:137], EMPTY)


def fold_kernel(start, *refs, n_q, q_at, n_in, parts, has_prior, message):
    n_h = len(parts)
    q_in, refs = refs[:n_q], refs[n_q:]
    k_in, refs = refs[:n_in], refs[n_in:]
    prior_in, refs = (refs[:n_q], refs[n_q:]) if has_prior else ((), refs)
    outs, refs = refs[:n_q], refs[n_q:]
    qs, ks, state, table, stretch_table, sems = refs
    pairs = [(q_in[i], qs.at[i]) for i in range(n_q)]
    for i, (source, row, _, half) in enumerate(parts):
        rows = SECOND_ROWS if half else FIRST_ROWS
        pairs.append((k_in[source].at[pl.ds(row, rows)], ks.at[i, pl.ds(0, rows)]))
    pairs += [(prior_in[i], state.at[i]) for i in range(len(prior_in))]
    copies = [pltpu.make_async_copy(a, b, sems.at[i]) for i, (a, b) in enumerate(pairs)]
    for made in copies:
        made.start()
    limit = start[0]
    ctx = lax.axis_index("ctx")
    k_ctx = [block_of(ctx, *offset) for offset in K_OFFSETS]
    q_ctx = [block_of(ctx, *offset) for offset in Q_OFFSETS]
    valid = [limit - k_ctx[slot] * PREFIX - half * HALF for _, _, slot, half in parts]
    count, edge, edge_valid = jnp.int32(0), jnp.int32(0), jnp.int32(0)
    for qi in range(n_q):
        for hi in range(n_h):
            table[count] = qi * n_h + hi
            count += (valid[hi] >= HALF).astype(jnp.int32)
    for hi in range(n_h):
        cut = (valid[hi] > 0) & (valid[hi] < HALF)
        edge, edge_valid = jnp.where(cut, hi, edge), jnp.where(cut, valid[hi], edge_valid)
    with_stretch = [(hi, slot) for hi, (_, _, slot, half) in enumerate(parts) if half == 0]
    stretches = jnp.int32(0)
    for qi in range(n_q):
        for hi, slot in with_stretch:
            apart = q_ctx[q_at + qi] - k_ctx[slot]
            stretch_table[stretches] = qi + 4 * hi + 64 * jnp.maximum(apart, 0)
            stretches += (apart >= 0).astype(jnp.int32)
    for made in copies:
        made.wait()
    largest_q = jnp.max(qs[:, ROWS:].astype(jnp.float32))
    largest_k = jnp.max(ks[:, NORM_AT:STRETCH_AT].astype(jnp.float32))
    safe = largest_q * largest_k <= SAFE
    if has_prior:
        safe &= jnp.max(jnp.abs(state[:, 136:])) == 0.0

    def raw_scores(qi, keys):
        return lax.dot_general(keys, qs[qi, :ROWS], (((1,), (1,)), ((), ())), preferred_element_type=jnp.float32)

    def values_of(hi):
        return jnp.concatenate([ks[hi, HALF + j : HALF + j + PAGE] for j in range(0, HALF, PAGE)], axis=1)

    def sublane_sums(weights):
        return jnp.sum(weights.reshape(weights.shape[0] // 8, 8, ROWS), axis=0)

    def fast_add(qi, raw, values, mask=None):
        weights = jnp.exp2(raw * SCALE2)
        if mask is not None:
            weights = jnp.where(mask, weights, 0.0)
        state[qi, 128:136] += sublane_sums(weights)
        state[qi, :128] += jnp.dot(values, weights.astype(jnp.bfloat16), preferred_element_type=jnp.float32)

    def key_minus_token():
        token = lax.broadcasted_iota(jnp.int32, (PAGE, ROWS), 1) & (PAGE - 1)
        return lax.broadcasted_iota(jnp.int32, (PAGE, ROWS), 0) - token

    def query_block(qi):
        block = q_ctx[q_at]
        for i in range(1, n_q):
            block = jnp.where(qi == i, q_ctx[q_at + i], block)
        return block

    def fold_stretch(t, c):
        task = stretch_table[t]
        qi, hi, apart = task % 4, task // 4 % 16, task // 64
        keys, values = ks[hi, STRETCH_AT : STRETCH_AT + PAGE], ks[hi, STRETCH_AT + PAGE : FIRST_ROWS]
        fast_add(qi, raw_scores(qi, keys), values, key_minus_token() <= apart * PAGE)
        return c

    def fold_edge(qi, c):
        mask = lax.broadcasted_iota(jnp.int32, (HALF, ROWS), 0) < edge_valid
        fast_add(qi, raw_scores(qi, ks[edge, :HALF]), values_of(edge), mask)
        return c

    def general_add(qi, keys, values, mask):
        scores = jnp.where(mask, raw_scores(qi, keys) * SCALE2, EMPTY)
        before = state[qi, 136:137]
        top = jnp.maximum(before, jnp.max(scores, axis=0, keepdims=True))
        factor = jnp.exp2(before - top)
        weights = jnp.where(mask, jnp.exp2(scores - top), 0.0)
        state[qi, 136:144] = jnp.broadcast_to(top, (8, ROWS))
        state[qi, 128:136] = state[qi, 128:136] * factor + sublane_sums(weights)
        state[qi, :128] = state[qi, :128] * factor + jnp.dot(
            values, weights.astype(jnp.bfloat16), preferred_element_type=jnp.float32
        )

    def general_part(hi, slot, half):
        def one(t, c):
            qi, j = t // 4, t % 4
            at = pl.multiple_of(j * PAGE, PAGE)
            keys = limit - k_ctx[slot] * PREFIX - half * HALF - at
            mask = lax.broadcasted_iota(jnp.int32, (PAGE, ROWS), 0) < keys
            general_add(qi, ks[hi, pl.ds(at, PAGE)], ks[hi, pl.ds(pl.multiple_of(HALF + at, PAGE), PAGE)], mask)
            return c

        lax.fori_loop(0, 4 * n_q, one, 0)

    def general_stretch(hi, slot):
        def one(qi, c):
            mask = key_minus_token() <= (query_block(qi) - k_ctx[slot]) * PAGE
            general_add(qi, ks[hi, STRETCH_AT : STRETCH_AT + PAGE], ks[hi, STRETCH_AT + PAGE : FIRST_ROWS], mask)
            return c

        lax.fori_loop(0, n_q, one, 0)

    if not has_prior:
        state[...] = jnp.zeros((n_q, STATE_ROWS, ROWS), jnp.float32)

    @pl.when(safe)
    def _():
        def add_entry(t):
            qi, hi = table[t] // n_h, table[t] % n_h
            fast_add(qi, raw_scores(qi, ks[hi, :HALF]), values_of(hi))

        def step(t, c):
            add_entry(2 * t)
            add_entry(2 * t + 1)
            return c

        lax.fori_loop(0, count // 2, step, 0)

        @pl.when(count % 2 == 1)
        def _():
            add_entry(count - 1)

        lax.fori_loop(0, jnp.where(edge_valid > 0, n_q, 0), fold_edge, 0)
        if with_stretch:
            lax.fori_loop(0, stretches, fold_stretch, 0)

    @pl.when(jnp.logical_not(safe))
    def _():
        for i in range(n_q):
            state[i, 136:] = jnp.broadcast_to(effective(state[i])[1], (8, ROWS))
        for hi, (_, _, slot, half) in enumerate(parts):
            general_part(hi, slot, half)
        for hi, slot in with_stretch:
            general_stretch(hi, slot)

    for i in range(n_q):
        if not message:
            outs[i][...] = state[i]
            continue
        total, top = effective(state[i])
        sent = jnp.where(top > EMPTY, 4.0 * jnp.ceil(top * 0.25), EMPTY)
        factor = jnp.exp2(top - sent)
        total = total * factor
        high = total.astype(jnp.bfloat16).astype(jnp.float32)
        row = lax.broadcasted_iota(jnp.int32, (16, ROWS), 0)
        tail = jnp.where(row == 0, high, jnp.where(row == 1, total - high, jnp.where(row == 2, sent, 0.0)))
        outs[i][:128] = (state[i, :128] * factor).astype(jnp.bfloat16)
        outs[i][128:] = tail.astype(jnp.bfloat16)


def whole_block(array, slot):
    return [(array, 0, slot, 0), (array, FIRST_ROWS, slot, 1)]


def fold(start, queries, q_at, halves, prior=(), message=False, cost=1.0, name="fold"):
    arrays = []
    for array, *_ in halves:
        if not any(array is other for other in arrays):
            arrays.append(array)
    parts = tuple(
        (next(i for i, other in enumerate(arrays) if other is array), row, slot, half)
        for array, row, slot, half in halves
    )
    n_q, n_h = len(queries), len(parts)
    anywhere = pl.BlockSpec(memory_space=pl.ANY)
    inputs = list(queries) + arrays + list(prior)
    work = 4 * n_q * n_h * ROWS * HALF * HEAD
    return pl.pallas_call(
        functools.partial(
            fold_kernel, n_q=n_q, q_at=q_at, n_in=len(arrays), parts=parts, has_prior=bool(prior), message=message
        ),
        out_shape=[jax.ShapeDtypeStruct((STATE_ROWS, ROWS), jnp.bfloat16 if message else jnp.float32)] * n_q,
        in_specs=[pl.BlockSpec(memory_space=pltpu.SMEM)] + [anywhere] * len(inputs),
        scratch_shapes=[
            pltpu.VMEM((n_q, QUERY_ROWS, HEAD), jnp.bfloat16),
            pltpu.VMEM((n_h, FIRST_ROWS, HEAD), jnp.bfloat16),
            pltpu.VMEM((n_q, STATE_ROWS, ROWS), jnp.float32),
            pltpu.SMEM((n_q * n_h + 1,), jnp.int32),
            pltpu.SMEM((n_q * n_h + 1,), jnp.int32),
            pltpu.SemaphoreType.DMA((len(inputs) + n_h,)),
        ],
        compiler_params=pltpu.CompilerParams(vmem_limit_bytes=48 << 20),
        cost_estimate=pl.CostEstimate(
            flops=int(2 * work * cost), transcendentals=0, bytes_accessed=int(n_h * 300000 * cost)
        ),
        name=name,
    )(start, *inputs)


def merge_kernel(own_ref, *refs):
    message_refs, out_ref = refs[:-1], refs[-1]
    total, top = effective(own_ref)
    tops, totals, sums = [top], [total], [own_ref[:128]]
    for ref in message_refs:
        tail = ref[128:].astype(jnp.float32)
        tops.append(tail[2:3])
        totals.append(tail[0:1] + tail[1:2])
        sums.append(ref[:128].astype(jnp.float32))
    top = functools.reduce(jnp.maximum, tops)
    factors = [jnp.exp2(t - top) for t in tops]
    total = functools.reduce(jnp.add, [t * f for t, f in zip(totals, factors)])
    inverse = 1.0 / total
    attended = functools.reduce(jnp.add, [s * (f * inverse) for s, f in zip(sums, factors)])
    for h in range(GROUP):
        columns = slice(h * HEAD, (h + 1) * HEAD)
        out_ref[0, :, columns] = attended[:, columns].T.astype(jnp.bfloat16)


def merge(own, messages):
    return pl.pallas_call(
        merge_kernel,
        out_shape=jax.ShapeDtypeStruct((1, PAGE, ROWS), jnp.bfloat16),
        compiler_params=pltpu.CompilerParams(vmem_limit_bytes=16 << 20),
        name="merge",
    )(own, *messages)


def received(page_rows, row_count):
    block = lax.axis_index("group") * 16 + lax.axis_index("ctx")
    kind = block % 4
    far = jnp.where(kind % 2 == 0, page_rows[(block + 16) % 32] - block * row_count, -1)
    source = jnp.where(kind == 3, block - block % 16 + (block + 8) % 16, jnp.maximum(block - 1, 0))
    near = jnp.where(kind >= 2, page_rows[source] - block * row_count, -1)
    return far, near


def scores_for(queries, keys):
    return lax.dot_general(queries, keys, (((1,), (1,)), ((), ())), preferred_element_type=jnp.float32) * SCALE2


def decode_kernel(page_rows, lengths, q_ref, cache_ref, draft_ref, out_ref, sum_ref, stat_ref, *, row_count):
    block_rows, rows, _ = q_ref.shape
    steps, limit = draft_ref.shape[2], cache_ref.shape[2]
    far, near = received(page_rows, row_count)
    for i in range(block_rows):
        r = pl.program_id(0) * block_rows + i
        length = lengths[r]
        first = jnp.where((r == far) | (r == near), PAGE, 0)
        queries = q_ref[i]
        position = lax.broadcasted_iota(jnp.int32, (rows, limit), 1)
        scores = scores_for(queries, cache_ref[0, i])
        scores = jnp.where((position >= first) & (position < length), scores, -jnp.inf)
        draft = scores_for(queries, draft_ref[0, i])
        step = lax.broadcasted_iota(jnp.int32, (rows, steps), 0) // GROUP
        draft = jnp.where(lax.broadcasted_iota(jnp.int32, (rows, steps), 1) <= step, draft, -jnp.inf)
        top = jnp.maximum(jnp.max(scores, axis=1, keepdims=True), jnp.max(draft, axis=1, keepdims=True))
        weights, draft_weights = jnp.exp2(scores - top), jnp.exp2(draft - top)
        total = jnp.sum(weights, axis=1, keepdims=True) + jnp.sum(draft_weights, axis=1, keepdims=True)
        summed = jnp.dot(weights.astype(jnp.bfloat16), cache_ref[1, i], preferred_element_type=jnp.float32)
        summed += jnp.dot(draft_weights.astype(jnp.bfloat16), draft_ref[1, i], preferred_element_type=jnp.float32)
        out_ref[i] = (summed / total).astype(jnp.bfloat16)
        sum_ref[i] = summed
        lane = lax.broadcasted_iota(jnp.int32, (rows, HEAD), 1)
        stat_ref[i] = jnp.where(lane == 0, total, top)


def decode(page_rows, lengths, queries, cache, draft):
    row_count, rows, _ = queries.shape
    steps, limit = draft.shape[2], cache.shape[2]
    block_rows = 4
    smem = pl.BlockSpec(memory_space=pltpu.SMEM)
    row_spec = pl.BlockSpec((block_rows, rows, HEAD), lambda r: (r, 0, 0))
    return pl.pallas_call(
        functools.partial(decode_kernel, row_count=row_count),
        grid=(row_count // block_rows,),
        out_shape=[jax.ShapeDtypeStruct(queries.shape, t) for t in (jnp.bfloat16, jnp.float32, jnp.float32)],
        in_specs=[
            smem,
            smem,
            row_spec,
            pl.BlockSpec((2, block_rows, limit, HEAD), lambda r: (0, r, 0, 0)),
            pl.BlockSpec((2, block_rows, steps, HEAD), lambda r: (0, r, 0, 0)),
        ],
        out_specs=[row_spec] * 3,
        compiler_params=pltpu.CompilerParams(vmem_limit_bytes=24 << 20),
        cost_estimate=pl.CostEstimate(flops=8 * row_count * rows * limit * HEAD, transcendentals=0, bytes_accessed=16 << 20),
        name="decode",
    )(page_rows, lengths, queries, pltpu.with_memory_space_constraint(cache, pltpu.HBM), draft)


def page_kernel(page_rows, q_ref, out_in, sum_ref, stat_ref, far_page, near_page, out_ref):
    row_count, rows, _ = q_ref.shape
    out_ref[...] = out_in[...]
    for r, page in zip(received(page_rows, row_count), (far_page, near_page)):

        @pl.when(r >= 0)
        def _():
            scores = scores_for(q_ref[r], page[0])
            before = stat_ref[r, :, 1:2]
            top = jnp.maximum(before, jnp.max(scores, axis=1, keepdims=True))
            factor = jnp.exp2(before - top)
            weights = jnp.exp2(scores - top)
            total = stat_ref[r, :, 0:1] * factor + jnp.sum(weights, axis=1, keepdims=True)
            summed = jnp.dot(weights.astype(jnp.bfloat16), page[1], preferred_element_type=jnp.float32)
            out_ref[r] = ((sum_ref[r] * factor + summed) / total).astype(jnp.bfloat16)


def with_pages(page_rows, queries, decoded, far_page, near_page):
    return pl.pallas_call(
        page_kernel,
        out_shape=jax.ShapeDtypeStruct(queries.shape, jnp.bfloat16),
        in_specs=[pl.BlockSpec(memory_space=pltpu.SMEM)] + [pl.BlockSpec(memory_space=pltpu.VMEM)] * 6,
        compiler_params=pltpu.CompilerParams(vmem_limit_bytes=16 << 20),
        name="pages",
    )(page_rows, queries, *decoded, far_page, near_page)


def near_pages():
    return [(c, c + 1) for c in range(1, 16, 4)] + [(c, (c + 8) % 16) for c in range(3, 16, 4)]


def on_device(
    stretch_query,
    prefix_keyvals,
    stretch_key_values,
    stretch_start,
    decode_query,
    draft_key_values,
    decode_cache,
    cache_lengths,
    page_rows,
):
    row_count, steps, _ = decode_query.shape
    send = lambda x, dz, dy: lax.ppermute(x, "ctx", xor_pairs(dz, dy))
    after = lambda x, *results: lax.optimization_barrier((x, *results))[0]
    query, own, own_first, own_second = prepare(stretch_query, prefix_keyvals, stretch_key_values)
    z_first = send(own_first, 2, 0)
    keys_y = send(own, 0, 1)
    query_y = send(query, 0, 3)
    query_z = send(query, 1, 0)
    query_d = send(query, 1, 3)
    z_second = send(own_second, 2, 0)
    d_first = send(z_first, 0, 1)

    decode_rows = decode_query.reshape(row_count, steps * GROUP, HEAD)
    decoded = decode(page_rows, cache_lengths, decode_rows, decode_cache, draft_key_values)
    start = after(stretch_start, *decoded)
    near_source = after(stretch_key_values[0], *decoded)
    near_page = lax.ppermute(near_source, "ctx", near_pages())
    far_page = lax.ppermute(near_source, ("group", "ctx"), [(n, (n + 16) % 32) for n in range(0, 32, 2)])

    others = [query_d, query_z, query_y]
    own_block, y_block = whole_block(own, 0), whole_block(keys_y, 1)
    z_block = [(z_first, 0, 2, 0), (z_second, 0, 2, 1)]
    states = fold(start, others, 1, own_block + y_block + z_block[:1], name="fold_first")
    z_second_late = after(z_second, *states)
    d_second = send(z_second_late, 0, 1)
    d_block = [(d_first, 0, 3, 0), (d_second, 0, 3, 1)]
    states = fold(
        start, others, 1, [(z_second_late, 0, 2, 1), d_block[0]], prior=states, name="fold_second"
    )
    messages = fold(start, others, 1, d_block[1:], prior=states, message=True, name="fold_third")
    from_d = send(messages[0], 1, 3)
    from_z = send(messages[1], 1, 0)
    from_y = send(messages[2], 0, 3)
    start = after(start, *messages)
    (final,) = fold(start, [query], 0, own_block + y_block + z_block + d_block, name="fold_own")
    decode_rows = after(decode_rows, final)
    decode_out = with_pages(page_rows, decode_rows, decoded, far_page, near_page).reshape(decode_query.shape)
    final = after(final, decode_out)
    prefill_out = merge(final, [from_y, from_z, from_d])
    return (prefill_out, decode_out)


def solution(mesh):
    return jax.shard_map(
        on_device,
        mesh=mesh,
        in_specs=(
            P("group", "ctx", "tp"),
            P("group", None, "ctx", "tp"),
            P("group", None, "ctx", "tp"),
            P("group"),
            P(("group", "ctx"), None, "tp"),
            P(None, ("group", "ctx"), None, "tp"),
            P(None, ("group", "ctx"), None, "tp"),
            P(("group", "ctx")),
            P(),
        ),
        out_specs=(P("group", "ctx", "tp"), P(("group", "ctx"), None, "tp")),
        check_vma=False,
    )
```

```python
import functools
import math

import jax
import jax.numpy as jnp
from jax import lax
from jax.experimental import pallas as pl
from jax.experimental.pallas import tpu as pltpu
from jax.sharding import PartitionSpec as P

HEAD = 128
GROUP = 8
ROWS = 1024
PREFIX = 1024
PAGE = 128
KEYS = PREFIX + PAGE
HALF = 512
NORM_AT = 2 * HALF
STRETCH_AT = NORM_AT + 16
FIRST_ROWS = STRETCH_AT + 2 * PAGE
SECOND_ROWS = STRETCH_AT
QUERY_ROWS = ROWS + 16
STATE_ROWS = 144
SCALE2 = math.log2(math.e) / math.sqrt(HEAD)
EMPTY = -1e30
SAFE = 75.0 * 75.0 * HEAD
Q_OFFSETS = ((0, 0), (1, 3), (1, 0), (0, 3))
K_OFFSETS = ((0, 0), (0, 1), (2, 0), (2, 1))


def xor_pairs(dz, dy):
    return [(z * 4 + y, (z ^ dz) * 4 + (y ^ dy)) for z in range(4) for y in range(4)]


def block_of(ctx, dz, dy):
    z, y = ctx // 4, ctx % 4
    flip = {0: lambda v: v, 1: lambda v: v + 1 - 2 * (v % 2), 2: lambda v: (v + 2) % 4, 3: lambda v: 3 - v}
    return flip[dz](z) * 4 + flip[dy](y)


def squares_max(rows):
    ones = jnp.ones((HEAD, HEAD), jnp.bfloat16)
    return jnp.max(jnp.dot(rows * rows, ones, preferred_element_type=jnp.float32))


def norm_rows(rows):
    return jnp.full((16, HEAD), squares_max(rows) * 1.04, jnp.float32).astype(jnp.bfloat16)


def prepare_kernel(query_hbm, prefix_hbm, stretch_hbm, query_msg, whole, first, second, keys, values, sems):
    copies = [
        (query_hbm.at[0, :, h * HEAD : (h + 1) * HEAD], query_msg.at[h * HEAD : (h + 1) * HEAD]) for h in range(GROUP)
    ]
    copies += [
        (prefix_hbm.at[0, 0], keys.at[:PREFIX]),
        (stretch_hbm.at[0, 0], keys.at[PREFIX:]),
        (prefix_hbm.at[0, 1], values.at[:PREFIX]),
        (stretch_hbm.at[0, 1], values.at[PREFIX:]),
    ]
    copies = [pltpu.make_async_copy(a, b, sems.at[i]) for i, (a, b) in enumerate(copies)]
    for made in copies:
        made.start()
    for made in copies[GROUP:]:
        made.wait()
    norms = norm_rows(keys[...])
    for at, base in ((0, 0), (HALF, FIRST_ROWS)):
        whole[base : base + HALF] = keys[at : at + HALF]
        for j in range(0, HALF, PAGE):
            whole[base + HALF + j : base + HALF + j + PAGE] = values[at + j : at + j + PAGE].T
        whole[base + NORM_AT : base + STRETCH_AT] = norms
    whole[STRETCH_AT : STRETCH_AT + PAGE] = keys[PREFIX:]
    whole[STRETCH_AT + PAGE : FIRST_ROWS] = values[PREFIX:].T
    first[...] = whole[:FIRST_ROWS]
    second[...] = whole[FIRST_ROWS:]
    for made in copies[:GROUP]:
        made.wait()
    query_msg[ROWS:] = norm_rows(query_msg[:ROWS])


def prepare(query, prefix, stretch):
    in_hbm = [pltpu.with_memory_space_constraint(x, pltpu.HBM) for x in (query, prefix, stretch)]
    return pl.pallas_call(
        prepare_kernel,
        out_shape=[
            jax.ShapeDtypeStruct((rows, HEAD), jnp.bfloat16)
            for rows in (QUERY_ROWS, FIRST_ROWS + SECOND_ROWS, FIRST_ROWS, SECOND_ROWS)
        ],
        in_specs=[pl.BlockSpec(memory_space=pl.ANY)] * 3,
        scratch_shapes=[
            pltpu.VMEM((KEYS, HEAD), jnp.bfloat16),
            pltpu.VMEM((KEYS, HEAD), jnp.bfloat16),
            pltpu.SemaphoreType.DMA((GROUP + 4,)),
        ],
        compiler_params=pltpu.CompilerParams(vmem_limit_bytes=16 << 20),
        name="prepare",
    )(*in_hbm)


def effective(state):
    total = jnp.sum(state[128:136], axis=0, keepdims=True)
    return total, jnp.where(total > 0.0, state[136:137], EMPTY)


def fold_kernel(start, *refs, n_q, q_at, n_in, parts, has_prior, message):
    n_h = len(parts)
    q_in, refs = refs[:n_q], refs[n_q:]
    k_in, refs = refs[:n_in], refs[n_in:]
    prior_in, refs = (refs[:n_q], refs[n_q:]) if has_prior else ((), refs)
    outs, refs = refs[:n_q], refs[n_q:]
    qs, ks, state, table, stretch_table, sems = refs
    pairs = [(q_in[i], qs.at[i]) for i in range(n_q)]
    for i, (source, row, _, half) in enumerate(parts):
        rows = SECOND_ROWS if half else FIRST_ROWS
        pairs.append((k_in[source].at[pl.ds(row, rows)], ks.at[i, pl.ds(0, rows)]))
    pairs += [(prior_in[i], state.at[i]) for i in range(len(prior_in))]
    copies = [pltpu.make_async_copy(a, b, sems.at[i]) for i, (a, b) in enumerate(pairs)]
    for made in copies:
        made.start()
    limit = start[0]
    ctx = lax.axis_index("ctx")
    k_ctx = [block_of(ctx, *offset) for offset in K_OFFSETS]
    q_ctx = [block_of(ctx, *offset) for offset in Q_OFFSETS]
    valid = [limit - k_ctx[slot] * PREFIX - half * HALF for _, _, slot, half in parts]
    count, edge, edge_valid = jnp.int32(0), jnp.int32(0), jnp.int32(0)
    for qi in range(n_q):
        for hi in range(n_h):
            table[count] = qi * n_h + hi
            count += (valid[hi] >= HALF).astype(jnp.int32)
    for hi in range(n_h):
        cut = (valid[hi] > 0) & (valid[hi] < HALF)
        edge, edge_valid = jnp.where(cut, hi, edge), jnp.where(cut, valid[hi], edge_valid)
    with_stretch = [(hi, slot) for hi, (_, _, slot, half) in enumerate(parts) if half == 0]
    stretches = jnp.int32(0)
    for qi in range(n_q):
        for hi, slot in with_stretch:
            apart = q_ctx[q_at + qi] - k_ctx[slot]
            stretch_table[stretches] = qi + 4 * hi + 64 * jnp.maximum(apart, 0)
            stretches += (apart >= 0).astype(jnp.int32)
    for made in copies:
        made.wait()
    largest_q = jnp.max(qs[:, ROWS:].astype(jnp.float32))
    largest_k = jnp.max(ks[:, NORM_AT:STRETCH_AT].astype(jnp.float32))
    safe = largest_q * largest_k <= SAFE
    if has_prior:
        safe &= jnp.max(jnp.abs(state[:, 136:])) == 0.0

    def raw_scores(qi, keys):
        return lax.dot_general(keys, qs[qi, :ROWS], (((1,), (1,)), ((), ())), preferred_element_type=jnp.float32)

    def values_of(hi):
        return jnp.concatenate([ks[hi, HALF + j : HALF + j + PAGE] for j in range(0, HALF, PAGE)], axis=1)

    def sublane_sums(weights):
        return jnp.sum(weights.reshape(weights.shape[0] // 8, 8, ROWS), axis=0)

    def fast_add(qi, raw, values, mask=None):
        weights = jnp.exp2(raw * SCALE2)
        if mask is not None:
            weights = jnp.where(mask, weights, 0.0)
        state[qi, 128:136] += sublane_sums(weights)
        state[qi, :128] += jnp.dot(values, weights.astype(jnp.bfloat16), preferred_element_type=jnp.float32)

    def key_minus_token():
        token = lax.broadcasted_iota(jnp.int32, (PAGE, ROWS), 1) & (PAGE - 1)
        return lax.broadcasted_iota(jnp.int32, (PAGE, ROWS), 0) - token

    def query_block(qi):
        block = q_ctx[q_at]
        for i in range(1, n_q):
            block = jnp.where(qi == i, q_ctx[q_at + i], block)
        return block

    def fold_stretch(t, c):
        task = stretch_table[t]
        qi, hi, apart = task % 4, task // 4 % 16, task // 64
        keys, values = ks[hi, STRETCH_AT : STRETCH_AT + PAGE], ks[hi, STRETCH_AT + PAGE : FIRST_ROWS]
        fast_add(qi, raw_scores(qi, keys), values, key_minus_token() <= apart * PAGE)
        return c

    def fold_edge(qi, c):
        mask = lax.broadcasted_iota(jnp.int32, (HALF, ROWS), 0) < edge_valid
        fast_add(qi, raw_scores(qi, ks[edge, :HALF]), values_of(edge), mask)
        return c

    def general_add(qi, keys, values, mask):
        scores = jnp.where(mask, raw_scores(qi, keys) * SCALE2, EMPTY)
        before = state[qi, 136:137]
        top = jnp.maximum(before, jnp.max(scores, axis=0, keepdims=True))
        factor = jnp.exp2(before - top)
        weights = jnp.where(mask, jnp.exp2(scores - top), 0.0)
        state[qi, 136:144] = jnp.broadcast_to(top, (8, ROWS))
        state[qi, 128:136] = state[qi, 128:136] * factor + sublane_sums(weights)
        state[qi, :128] = state[qi, :128] * factor + jnp.dot(
            values, weights.astype(jnp.bfloat16), preferred_element_type=jnp.float32
        )

    def general_part(hi, slot, half):
        def one(t, c):
            qi, j = t // 4, t % 4
            at = pl.multiple_of(j * PAGE, PAGE)
            keys = limit - k_ctx[slot] * PREFIX - half * HALF - at
            mask = lax.broadcasted_iota(jnp.int32, (PAGE, ROWS), 0) < keys
            general_add(qi, ks[hi, pl.ds(at, PAGE)], ks[hi, pl.ds(pl.multiple_of(HALF + at, PAGE), PAGE)], mask)
            return c

        lax.fori_loop(0, 4 * n_q, one, 0)

    def general_stretch(hi, slot):
        def one(qi, c):
            mask = key_minus_token() <= (query_block(qi) - k_ctx[slot]) * PAGE
            general_add(qi, ks[hi, STRETCH_AT : STRETCH_AT + PAGE], ks[hi, STRETCH_AT + PAGE : FIRST_ROWS], mask)
            return c

        lax.fori_loop(0, n_q, one, 0)

    if not has_prior:
        state[...] = jnp.zeros((n_q, STATE_ROWS, ROWS), jnp.float32)

    @pl.when(safe)
    def _():
        def add_entry(t):
            qi, hi = table[t] // n_h, table[t] % n_h
            fast_add(qi, raw_scores(qi, ks[hi, :HALF]), values_of(hi))

        def step(t, c):
            add_entry(2 * t)
            add_entry(2 * t + 1)
            return c

        lax.fori_loop(0, count // 2, step, 0)

        @pl.when(count % 2 == 1)
        def _():
            add_entry(count - 1)

        lax.fori_loop(0, jnp.where(edge_valid > 0, n_q, 0), fold_edge, 0)
        if with_stretch:
            lax.fori_loop(0, stretches, fold_stretch, 0)

    @pl.when(jnp.logical_not(safe))
    def _():
        for i in range(n_q):
            state[i, 136:] = jnp.broadcast_to(effective(state[i])[1], (8, ROWS))
        for hi, (_, _, slot, half) in enumerate(parts):
            general_part(hi, slot, half)
        for hi, slot in with_stretch:
            general_stretch(hi, slot)

    for i in range(n_q):
        if not message:
            outs[i][...] = state[i]
            continue
        total, top = effective(state[i])
        sent = jnp.where(top > EMPTY, 4.0 * jnp.ceil(top * 0.25), EMPTY)
        factor = jnp.exp2(top - sent)
        total = total * factor
        high = total.astype(jnp.bfloat16).astype(jnp.float32)
        row = lax.broadcasted_iota(jnp.int32, (16, ROWS), 0)
        tail = jnp.where(row == 0, high, jnp.where(row == 1, total - high, jnp.where(row == 2, sent, 0.0)))
        outs[i][:128] = (state[i, :128] * factor).astype(jnp.bfloat16)
        outs[i][128:] = tail.astype(jnp.bfloat16)


def whole_block(array, slot):
    return [(array, 0, slot, 0), (array, FIRST_ROWS, slot, 1)]


def fold(start, queries, q_at, halves, prior=(), message=False, cost=1.0, name="fold"):
    arrays = []
    for array, *_ in halves:
        if not any(array is other for other in arrays):
            arrays.append(array)
    parts = tuple(
        (next(i for i, other in enumerate(arrays) if other is array), row, slot, half)
        for array, row, slot, half in halves
    )
    n_q, n_h = len(queries), len(parts)
    anywhere = pl.BlockSpec(memory_space=pl.ANY)
    inputs = list(queries) + arrays + list(prior)
    work = 4 * n_q * n_h * ROWS * HALF * HEAD
    return pl.pallas_call(
        functools.partial(
            fold_kernel, n_q=n_q, q_at=q_at, n_in=len(arrays), parts=parts, has_prior=bool(prior), message=message
        ),
        out_shape=[jax.ShapeDtypeStruct((STATE_ROWS, ROWS), jnp.bfloat16 if message else jnp.float32)] * n_q,
        in_specs=[pl.BlockSpec(memory_space=pltpu.SMEM)] + [anywhere] * len(inputs),
        scratch_shapes=[
            pltpu.VMEM((n_q, QUERY_ROWS, HEAD), jnp.bfloat16),
            pltpu.VMEM((n_h, FIRST_ROWS, HEAD), jnp.bfloat16),
            pltpu.VMEM((n_q, STATE_ROWS, ROWS), jnp.float32),
            pltpu.SMEM((n_q * n_h + 1,), jnp.int32),
            pltpu.SMEM((n_q * n_h + 1,), jnp.int32),
            pltpu.SemaphoreType.DMA((len(inputs) + n_h,)),
        ],
        compiler_params=pltpu.CompilerParams(vmem_limit_bytes=48 << 20),
        cost_estimate=pl.CostEstimate(
            flops=int(2 * work * cost), transcendentals=0, bytes_accessed=int(n_h * 300000 * cost)
        ),
        name=name,
    )(start, *inputs)


def merge_kernel(own_ref, *refs):
    message_refs, out_ref = refs[:-1], refs[-1]
    total, top = effective(own_ref)
    tops, totals, sums = [top], [total], [own_ref[:128]]
    for ref in message_refs:
        tail = ref[128:].astype(jnp.float32)
        tops.append(tail[2:3])
        totals.append(tail[0:1] + tail[1:2])
        sums.append(ref[:128].astype(jnp.float32))
    top = functools.reduce(jnp.maximum, tops)
    factors = [jnp.exp2(t - top) for t in tops]
    total = functools.reduce(jnp.add, [t * f for t, f in zip(totals, factors)])
    inverse = 1.0 / total
    attended = functools.reduce(jnp.add, [s * (f * inverse) for s, f in zip(sums, factors)])
    for h in range(GROUP):
        columns = slice(h * HEAD, (h + 1) * HEAD)
        out_ref[0, :, columns] = attended[:, columns].T.astype(jnp.bfloat16)


def merge(own, messages):
    return pl.pallas_call(
        merge_kernel,
        out_shape=jax.ShapeDtypeStruct((1, PAGE, ROWS), jnp.bfloat16),
        compiler_params=pltpu.CompilerParams(vmem_limit_bytes=16 << 20),
        name="merge",
    )(own, *messages)


def received(page_rows, row_count):
    block = lax.axis_index("group") * 16 + lax.axis_index("ctx")
    kind = block % 4
    far = jnp.where(kind % 2 == 0, page_rows[(block + 16) % 32] - block * row_count, -1)
    source = jnp.where(kind == 3, block - block % 16 + (block + 8) % 16, jnp.maximum(block - 1, 0))
    near = jnp.where(kind >= 2, page_rows[source] - block * row_count, -1)
    return far, near


def scores_for(queries, keys):
    return lax.dot_general(queries, keys, (((1,), (1,)), ((), ())), preferred_element_type=jnp.float32) * SCALE2


def decode_kernel(page_rows, lengths, q_ref, cache_ref, draft_ref, out_ref, sum_ref, stat_ref, *, row_count):
    block_rows, rows, _ = q_ref.shape
    steps, limit = draft_ref.shape[2], cache_ref.shape[2]
    far, near = received(page_rows, row_count)
    every = range(block_rows)
    cached = [scores_for(q_ref[i], cache_ref[0, i]) for i in every]
    drafted = [scores_for(q_ref[i], draft_ref[0, i]) for i in every]
    position = lax.broadcasted_iota(jnp.int32, (rows, limit), 1)
    step = lax.broadcasted_iota(jnp.int32, (rows, steps), 0) // GROUP
    causal = lax.broadcasted_iota(jnp.int32, (rows, steps), 1) <= step
    lane = lax.broadcasted_iota(jnp.int32, (rows, HEAD), 1)
    pieces = []
    for i in every:
        r = pl.program_id(0) * block_rows + i
        first = jnp.where((r == far) | (r == near), PAGE, 0)
        scores = jnp.where((position >= first) & (position < lengths[r]), cached[i], -jnp.inf)
        draft = jnp.where(causal, drafted[i], -jnp.inf)
        top = jnp.maximum(jnp.max(scores, axis=1, keepdims=True), jnp.max(draft, axis=1, keepdims=True))
        weights, draft_weights = jnp.exp2(scores - top), jnp.exp2(draft - top)
        total = jnp.sum(weights, axis=1, keepdims=True) + jnp.sum(draft_weights, axis=1, keepdims=True)
        stat_ref[i] = jnp.where(lane == 0, total, top)
        pieces.append((weights.astype(jnp.bfloat16), draft_weights.astype(jnp.bfloat16), total))
    for i, (weights, draft_weights, total) in enumerate(pieces):
        summed = jnp.dot(weights, cache_ref[1, i], preferred_element_type=jnp.float32)
        summed += jnp.dot(draft_weights, draft_ref[1, i], preferred_element_type=jnp.float32)
        out_ref[i] = (summed / total).astype(jnp.bfloat16)
        sum_ref[i] = summed


def decode(page_rows, lengths, queries, cache, draft):
    row_count, rows, _ = queries.shape
    steps, limit = draft.shape[2], cache.shape[2]
    block_rows = 8
    smem = pl.BlockSpec(memory_space=pltpu.SMEM)
    row_spec = pl.BlockSpec((block_rows, rows, HEAD), lambda r: (r, 0, 0))
    return pl.pallas_call(
        functools.partial(decode_kernel, row_count=row_count),
        grid=(row_count // block_rows,),
        out_shape=[jax.ShapeDtypeStruct(queries.shape, t) for t in (jnp.bfloat16, jnp.float32, jnp.float32)],
        in_specs=[
            smem,
            smem,
            row_spec,
            pl.BlockSpec((2, block_rows, limit, HEAD), lambda r: (0, r, 0, 0)),
            pl.BlockSpec((2, block_rows, steps, HEAD), lambda r: (0, r, 0, 0)),
        ],
        out_specs=[row_spec] * 3,
        compiler_params=pltpu.CompilerParams(vmem_limit_bytes=32 << 20),
        cost_estimate=pl.CostEstimate(flops=8 * row_count * rows * limit * HEAD, transcendentals=0, bytes_accessed=16 << 20),
        name="decode",
    )(page_rows, lengths, queries, *(pltpu.with_memory_space_constraint(x, pltpu.HBM) for x in (cache, draft)))


def page_kernel(page_rows, q_ref, out_in, sum_ref, stat_ref, far_page, near_page, out_ref):
    row_count, rows, _ = q_ref.shape
    out_ref[...] = out_in[...]
    for r, page in zip(received(page_rows, row_count), (far_page, near_page)):

        @pl.when(r >= 0)
        def _():
            scores = scores_for(q_ref[r], page[0])
            before = stat_ref[r, :, 1:2]
            top = jnp.maximum(before, jnp.max(scores, axis=1, keepdims=True))
            factor = jnp.exp2(before - top)
            weights = jnp.exp2(scores - top)
            total = stat_ref[r, :, 0:1] * factor + jnp.sum(weights, axis=1, keepdims=True)
            summed = jnp.dot(weights.astype(jnp.bfloat16), page[1], preferred_element_type=jnp.float32)
            out_ref[r] = ((sum_ref[r] * factor + summed) / total).astype(jnp.bfloat16)


def with_pages(page_rows, queries, decoded, far_page, near_page):
    return pl.pallas_call(
        page_kernel,
        out_shape=jax.ShapeDtypeStruct(queries.shape, jnp.bfloat16),
        in_specs=[pl.BlockSpec(memory_space=pltpu.SMEM)] + [pl.BlockSpec(memory_space=pltpu.VMEM)] * 6,
        compiler_params=pltpu.CompilerParams(vmem_limit_bytes=16 << 20),
        name="pages",
    )(page_rows, queries, *decoded, far_page, near_page)


def near_pages():
    return [(c, c + 1) for c in range(1, 16, 4)] + [(c, (c + 8) % 16) for c in range(3, 16, 4)]


def on_device(
    stretch_query,
    prefix_keyvals,
    stretch_key_values,
    stretch_start,
    decode_query,
    draft_key_values,
    decode_cache,
    cache_lengths,
    page_rows,
):
    row_count, steps, _ = decode_query.shape
    send = lambda x, dz, dy: lax.ppermute(x, "ctx", xor_pairs(dz, dy))
    after = lambda x, *results: lax.optimization_barrier((x, *results))[0]
    query, own, own_first, own_second = prepare(stretch_query, prefix_keyvals, stretch_key_values)
    z_first = send(own_first, 2, 0)
    keys_y = send(own, 0, 1)
    query_y = send(query, 0, 3)
    query_z = send(query, 1, 0)
    query_d = send(query, 1, 3)
    d_first = send(z_first, 0, 1)

    decode_rows = decode_query.reshape(row_count, steps * GROUP, HEAD)
    decoded = decode(page_rows, cache_lengths, decode_rows, decode_cache, draft_key_values)
    start = after(stretch_start, *decoded)
    z_second = send(after(own_second, keys_y, *decoded), 2, 0)
    d_second = send(z_second, 0, 1)
    near_source = after(stretch_key_values[0], z_first, *decoded)
    near_page = lax.ppermute(near_source, "ctx", near_pages())
    far_page = lax.ppermute(near_source, ("group", "ctx"), [(n, (n + 16) % 32) for n in range(0, 32, 2)])

    others = [query_d, query_z, query_y]
    near = whole_block(own, 0) + whole_block(keys_y, 1) + [(z_first, 0, 2, 0), (z_second, 0, 2, 1)]
    far = [(d_first, 0, 3, 0), (d_second, 0, 3, 1)]
    states = fold(start, others, 1, near, name="fold_near")
    messages = fold(start, others, 1, far, prior=states, message=True, name="fold_far")
    from_d = send(messages[0], 1, 3)
    from_z = send(messages[1], 1, 0)
    from_y = send(messages[2], 0, 3)
    start = after(start, *messages)
    (final,) = fold(start, [query], 0, near + far, name="fold_own")
    decode_rows = after(decode_rows, final)
    decode_out = with_pages(page_rows, decode_rows, decoded, far_page, near_page).reshape(decode_query.shape)
    final = after(final, decode_out)
    prefill_out = merge(final, [from_y, from_z, from_d])
    return (prefill_out, decode_out)


def solution(mesh):
    return jax.shard_map(
        on_device,
        mesh=mesh,
        in_specs=(
            P("group", "ctx", "tp"),
            P("group", None, "ctx", "tp"),
            P("group", None, "ctx", "tp"),
            P("group"),
            P(("group", "ctx"), None, "tp"),
            P(None, ("group", "ctx"), None, "tp"),
            P(None, ("group", "ctx"), None, "tp"),
            P(("group", "ctx")),
            P(),
        ),
        out_specs=(P("group", "ctx", "tp"), P(("group", "ctx"), None, "tp")),
        check_vma=False,
    )
```

```python
import functools
import math

import jax
import jax.numpy as jnp
from jax import lax
from jax.experimental import pallas as pl
from jax.experimental.pallas import tpu as pltpu
from jax.sharding import PartitionSpec as P

HEAD = 128
GROUP = 8
ROWS = 1024
PREFIX = 1024
PAGE = 128
KEYS = PREFIX + PAGE
HALF = 512
NORM_AT = 2 * HALF
STRETCH_AT = NORM_AT + 16
FIRST_ROWS = STRETCH_AT + 2 * PAGE
SECOND_ROWS = STRETCH_AT
QUERY_ROWS = ROWS + 16
STATE_ROWS = 144
SCALE2 = math.log2(math.e) / math.sqrt(HEAD)
EMPTY = -1e30
SAFE = 75.0 * 75.0 * HEAD
Q_OFFSETS = ((0, 0), (1, 3), (1, 0), (0, 3))
K_OFFSETS = ((0, 0), (0, 1), (2, 0), (2, 1))


def xor_pairs(dz, dy):
    return [(z * 4 + y, (z ^ dz) * 4 + (y ^ dy)) for z in range(4) for y in range(4)]


def block_of(ctx, dz, dy):
    z, y = ctx // 4, ctx % 4
    flip = {0: lambda v: v, 1: lambda v: v + 1 - 2 * (v % 2), 2: lambda v: (v + 2) % 4, 3: lambda v: 3 - v}
    return flip[dz](z) * 4 + flip[dy](y)


def squares_max(rows):
    ones = jnp.ones((HEAD, HEAD), jnp.bfloat16)
    return jnp.max(jnp.dot(rows * rows, ones, preferred_element_type=jnp.float32))


def norm_rows(rows):
    return jnp.full((16, HEAD), squares_max(rows) * 1.04, jnp.float32).astype(jnp.bfloat16)


def prepare_kernel(query_hbm, prefix_hbm, stretch_hbm, query_msg, whole, first, second, keys, values, sems):
    copies = [
        (query_hbm.at[0, :, h * HEAD : (h + 1) * HEAD], query_msg.at[h * HEAD : (h + 1) * HEAD]) for h in range(GROUP)
    ]
    copies += [
        (prefix_hbm.at[0, 0], keys.at[:PREFIX]),
        (stretch_hbm.at[0, 0], keys.at[PREFIX:]),
        (prefix_hbm.at[0, 1], values.at[:PREFIX]),
        (stretch_hbm.at[0, 1], values.at[PREFIX:]),
    ]
    copies = [pltpu.make_async_copy(a, b, sems.at[i]) for i, (a, b) in enumerate(copies)]
    for made in copies:
        made.start()
    for made in copies[GROUP:]:
        made.wait()
    norms = norm_rows(keys[...])
    for at, base in ((0, 0), (HALF, FIRST_ROWS)):
        whole[base : base + HALF] = keys[at : at + HALF]
        for j in range(0, HALF, PAGE):
            whole[base + HALF + j : base + HALF + j + PAGE] = values[at + j : at + j + PAGE].T
        whole[base + NORM_AT : base + STRETCH_AT] = norms
    whole[STRETCH_AT : STRETCH_AT + PAGE] = keys[PREFIX:]
    whole[STRETCH_AT + PAGE : FIRST_ROWS] = values[PREFIX:].T
    first[...] = whole[:FIRST_ROWS]
    second[...] = whole[FIRST_ROWS:]
    for made in copies[:GROUP]:
        made.wait()
    query_msg[ROWS:] = norm_rows(query_msg[:ROWS])


def prepare(query, prefix, stretch):
    in_hbm = [pltpu.with_memory_space_constraint(x, pltpu.HBM) for x in (query, prefix, stretch)]
    return pl.pallas_call(
        prepare_kernel,
        out_shape=[
            jax.ShapeDtypeStruct((rows, HEAD), jnp.bfloat16)
            for rows in (QUERY_ROWS, FIRST_ROWS + SECOND_ROWS, FIRST_ROWS, SECOND_ROWS)
        ],
        in_specs=[pl.BlockSpec(memory_space=pl.ANY)] * 3,
        scratch_shapes=[
            pltpu.VMEM((KEYS, HEAD), jnp.bfloat16),
            pltpu.VMEM((KEYS, HEAD), jnp.bfloat16),
            pltpu.SemaphoreType.DMA((GROUP + 4,)),
        ],
        compiler_params=pltpu.CompilerParams(vmem_limit_bytes=16 << 20),
        name="prepare",
    )(*in_hbm)


def effective(state):
    total = jnp.sum(state[128:136], axis=0, keepdims=True)
    return total, jnp.where(total > 0.0, state[136:137], EMPTY)


def fold_kernel(start, *refs, n_q, q_at, n_in, parts, has_prior, message):
    n_h = len(parts)
    q_in, refs = refs[:n_q], refs[n_q:]
    k_in, refs = refs[:n_in], refs[n_in:]
    prior_in, refs = (refs[:n_q], refs[n_q:]) if has_prior else ((), refs)
    outs, refs = refs[:n_q], refs[n_q:]
    qs, ks, state, table, stretch_table, sems = refs
    pairs = [(q_in[i], qs.at[i]) for i in range(n_q)]
    for i, (source, row, _, half) in enumerate(parts):
        rows = SECOND_ROWS if half else FIRST_ROWS
        pairs.append((k_in[source].at[pl.ds(row, rows)], ks.at[i, pl.ds(0, rows)]))
    pairs += [(prior_in[i], state.at[i]) for i in range(len(prior_in))]
    copies = [pltpu.make_async_copy(a, b, sems.at[i]) for i, (a, b) in enumerate(pairs)]
    for made in copies:
        made.start()
    limit = start[0]
    ctx = lax.axis_index("ctx")
    k_ctx = [block_of(ctx, *offset) for offset in K_OFFSETS]
    q_ctx = [block_of(ctx, *offset) for offset in Q_OFFSETS]
    valid = [limit - k_ctx[slot] * PREFIX - half * HALF for _, _, slot, half in parts]
    count, edge, edge_valid = jnp.int32(0), jnp.int32(0), jnp.int32(0)
    for qi in range(n_q):
        for hi in range(n_h):
            table[count] = qi * n_h + hi
            count += (valid[hi] >= HALF).astype(jnp.int32)
    for hi in range(n_h):
        cut = (valid[hi] > 0) & (valid[hi] < HALF)
        edge, edge_valid = jnp.where(cut, hi, edge), jnp.where(cut, valid[hi], edge_valid)
    with_stretch = [(hi, slot) for hi, (_, _, slot, half) in enumerate(parts) if half == 0]
    stretches = jnp.int32(0)
    for qi in range(n_q):
        for hi, slot in with_stretch:
            apart = q_ctx[q_at + qi] - k_ctx[slot]
            stretch_table[stretches] = qi + 4 * hi + 64 * jnp.maximum(apart, 0)
            stretches += (apart >= 0).astype(jnp.int32)
    for made in copies:
        made.wait()
    largest_q = jnp.max(qs[:, ROWS:].astype(jnp.float32))
    largest_k = jnp.max(ks[:, NORM_AT:STRETCH_AT].astype(jnp.float32))
    safe = largest_q * largest_k <= SAFE
    if has_prior:
        safe &= jnp.max(jnp.abs(state[:, 136:])) == 0.0

    def raw_scores(qi, keys):
        return lax.dot_general(keys, qs[qi, :ROWS], (((1,), (1,)), ((), ())), preferred_element_type=jnp.float32)

    def values_of(hi):
        return jnp.concatenate([ks[hi, HALF + j : HALF + j + PAGE] for j in range(0, HALF, PAGE)], axis=1)

    def sublane_sums(weights):
        return jnp.sum(weights.reshape(weights.shape[0] // 8, 8, ROWS), axis=0)

    def fast_add(qi, raw, values, mask=None):
        weights = jnp.exp2(raw * SCALE2)
        if mask is not None:
            weights = jnp.where(mask, weights, 0.0)
        state[qi, 128:136] += sublane_sums(weights)
        state[qi, :128] += jnp.dot(values, weights.astype(jnp.bfloat16), preferred_element_type=jnp.float32)

    def key_minus_token():
        token = lax.broadcasted_iota(jnp.int32, (PAGE, ROWS), 1) & (PAGE - 1)
        return lax.broadcasted_iota(jnp.int32, (PAGE, ROWS), 0) - token

    def query_block(qi):
        block = q_ctx[q_at]
        for i in range(1, n_q):
            block = jnp.where(qi == i, q_ctx[q_at + i], block)
        return block

    def fold_stretch(t, c):
        task = stretch_table[t]
        qi, hi, apart = task % 4, task // 4 % 16, task // 64
        keys, values = ks[hi, STRETCH_AT : STRETCH_AT + PAGE], ks[hi, STRETCH_AT + PAGE : FIRST_ROWS]
        fast_add(qi, raw_scores(qi, keys), values, key_minus_token() <= apart * PAGE)
        return c

    def fold_edge(qi, c):
        mask = lax.broadcasted_iota(jnp.int32, (HALF, ROWS), 0) < edge_valid
        fast_add(qi, raw_scores(qi, ks[edge, :HALF]), values_of(edge), mask)
        return c

    def general_add(qi, keys, values, mask):
        scores = jnp.where(mask, raw_scores(qi, keys) * SCALE2, EMPTY)
        before = state[qi, 136:137]
        top = jnp.maximum(before, jnp.max(scores, axis=0, keepdims=True))
        factor = jnp.exp2(before - top)
        weights = jnp.where(mask, jnp.exp2(scores - top), 0.0)
        state[qi, 136:144] = jnp.broadcast_to(top, (8, ROWS))
        state[qi, 128:136] = state[qi, 128:136] * factor + sublane_sums(weights)
        state[qi, :128] = state[qi, :128] * factor + jnp.dot(
            values, weights.astype(jnp.bfloat16), preferred_element_type=jnp.float32
        )

    def general_part(hi, slot, half):
        def one(t, c):
            qi, j = t // 4, t % 4
            at = pl.multiple_of(j * PAGE, PAGE)
            keys = limit - k_ctx[slot] * PREFIX - half * HALF - at
            mask = lax.broadcasted_iota(jnp.int32, (PAGE, ROWS), 0) < keys
            general_add(qi, ks[hi, pl.ds(at, PAGE)], ks[hi, pl.ds(pl.multiple_of(HALF + at, PAGE), PAGE)], mask)
            return c

        lax.fori_loop(0, 4 * n_q, one, 0)

    def general_stretch(hi, slot):
        def one(qi, c):
            mask = key_minus_token() <= (query_block(qi) - k_ctx[slot]) * PAGE
            general_add(qi, ks[hi, STRETCH_AT : STRETCH_AT + PAGE], ks[hi, STRETCH_AT + PAGE : FIRST_ROWS], mask)
            return c

        lax.fori_loop(0, n_q, one, 0)

    if not has_prior:
        state[...] = jnp.zeros((n_q, STATE_ROWS, ROWS), jnp.float32)

    @pl.when(safe)
    def _():
        def add_entry(t):
            qi, hi = table[t] // n_h, table[t] % n_h
            fast_add(qi, raw_scores(qi, ks[hi, :HALF]), values_of(hi))

        def step(t, c):
            add_entry(2 * t)
            add_entry(2 * t + 1)
            return c

        lax.fori_loop(0, count // 2, step, 0)

        @pl.when(count % 2 == 1)
        def _():
            add_entry(count - 1)

        lax.fori_loop(0, jnp.where(edge_valid > 0, n_q, 0), fold_edge, 0)
        if with_stretch:
            lax.fori_loop(0, stretches, fold_stretch, 0)

    @pl.when(jnp.logical_not(safe))
    def _():
        for i in range(n_q):
            state[i, 136:] = jnp.broadcast_to(effective(state[i])[1], (8, ROWS))
        for hi, (_, _, slot, half) in enumerate(parts):
            general_part(hi, slot, half)
        for hi, slot in with_stretch:
            general_stretch(hi, slot)

    for i in range(n_q):
        if not message:
            outs[i][...] = state[i]
            continue
        total, top = effective(state[i])
        sent = jnp.where(top > EMPTY, 4.0 * jnp.ceil(top * 0.25), EMPTY)
        factor = jnp.exp2(top - sent)
        total = total * factor
        high = total.astype(jnp.bfloat16).astype(jnp.float32)
        row = lax.broadcasted_iota(jnp.int32, (16, ROWS), 0)
        tail = jnp.where(row == 0, high, jnp.where(row == 1, total - high, jnp.where(row == 2, sent, 0.0)))
        outs[i][:128] = (state[i, :128] * factor).astype(jnp.bfloat16)
        outs[i][128:] = tail.astype(jnp.bfloat16)


def whole_block(array, slot):
    return [(array, 0, slot, 0), (array, FIRST_ROWS, slot, 1)]


def fold(start, queries, q_at, halves, prior=(), message=False, cost=1.0, name="fold"):
    arrays = []
    for array, *_ in halves:
        if not any(array is other for other in arrays):
            arrays.append(array)
    parts = tuple(
        (next(i for i, other in enumerate(arrays) if other is array), row, slot, half)
        for array, row, slot, half in halves
    )
    n_q, n_h = len(queries), len(parts)
    anywhere = pl.BlockSpec(memory_space=pl.ANY)
    inputs = list(queries) + arrays + list(prior)
    work = 4 * n_q * n_h * ROWS * HALF * HEAD
    return pl.pallas_call(
        functools.partial(
            fold_kernel, n_q=n_q, q_at=q_at, n_in=len(arrays), parts=parts, has_prior=bool(prior), message=message
        ),
        out_shape=[jax.ShapeDtypeStruct((STATE_ROWS, ROWS), jnp.bfloat16 if message else jnp.float32)] * n_q,
        in_specs=[pl.BlockSpec(memory_space=pltpu.SMEM)] + [anywhere] * len(inputs),
        scratch_shapes=[
            pltpu.VMEM((n_q, QUERY_ROWS, HEAD), jnp.bfloat16),
            pltpu.VMEM((n_h, FIRST_ROWS, HEAD), jnp.bfloat16),
            pltpu.VMEM((n_q, STATE_ROWS, ROWS), jnp.float32),
            pltpu.SMEM((n_q * n_h + 1,), jnp.int32),
            pltpu.SMEM((n_q * n_h + 1,), jnp.int32),
            pltpu.SemaphoreType.DMA((len(inputs) + n_h,)),
        ],
        compiler_params=pltpu.CompilerParams(vmem_limit_bytes=48 << 20),
        cost_estimate=pl.CostEstimate(
            flops=int(2 * work * cost), transcendentals=0, bytes_accessed=int(n_h * 300000 * cost)
        ),
        name=name,
    )(start, *inputs)


def merge_kernel(own_ref, *refs):
    message_refs, out_ref = refs[:-1], refs[-1]
    total, top = effective(own_ref)
    tops, totals, sums = [top], [total], [own_ref[:128]]
    for ref in message_refs:
        tail = ref[128:].astype(jnp.float32)
        tops.append(tail[2:3])
        totals.append(tail[0:1] + tail[1:2])
        sums.append(ref[:128].astype(jnp.float32))
    top = functools.reduce(jnp.maximum, tops)
    factors = [jnp.exp2(t - top) for t in tops]
    total = functools.reduce(jnp.add, [t * f for t, f in zip(totals, factors)])
    inverse = 1.0 / total
    attended = functools.reduce(jnp.add, [s * (f * inverse) for s, f in zip(sums, factors)])
    for h in range(GROUP):
        columns = slice(h * HEAD, (h + 1) * HEAD)
        out_ref[0, :, columns] = attended[:, columns].T.astype(jnp.bfloat16)


def merge(own, messages):
    return pl.pallas_call(
        merge_kernel,
        out_shape=jax.ShapeDtypeStruct((1, PAGE, ROWS), jnp.bfloat16),
        compiler_params=pltpu.CompilerParams(vmem_limit_bytes=16 << 20),
        name="merge",
    )(own, *messages)


def received(page_rows, row_count):
    block = lax.axis_index("group") * 16 + lax.axis_index("ctx")
    kind = block % 4
    far = jnp.where(kind % 2 == 0, page_rows[(block + 16) % 32] - block * row_count, -1)
    source = jnp.where(kind == 3, block - block % 16 + (block + 8) % 16, jnp.maximum(block - 1, 0))
    near = jnp.where(kind >= 2, page_rows[source] - block * row_count, -1)
    return far, near


def scores_for(queries, keys):
    return lax.dot_general(queries, keys, (((1,), (1,)), ((), ())), preferred_element_type=jnp.float32) * SCALE2


def decode_kernel(page_rows, lengths, q_ref, cache_ref, draft_ref, out_ref, sum_ref, stat_ref, *, row_count):
    block_rows, rows, _ = q_ref.shape
    steps, limit = draft_ref.shape[2], cache_ref.shape[2]
    far, near = received(page_rows, row_count)
    every = range(block_rows)
    cached = [scores_for(q_ref[i], cache_ref[0, i]) for i in every]
    drafted = [scores_for(q_ref[i], draft_ref[0, i]) for i in every]
    position = lax.broadcasted_iota(jnp.int32, (rows, limit), 1)
    step = lax.broadcasted_iota(jnp.int32, (rows, steps), 0) // GROUP
    causal = lax.broadcasted_iota(jnp.int32, (rows, steps), 1) <= step
    lane = lax.broadcasted_iota(jnp.int32, (rows, HEAD), 1)
    pieces = []
    for i in every:
        r = pl.program_id(0) * block_rows + i
        first = jnp.where((r == far) | (r == near), PAGE, 0)
        scores = jnp.where((position >= first) & (position < lengths[r]), cached[i], -jnp.inf)
        draft = jnp.where(causal, drafted[i], -jnp.inf)
        top = jnp.maximum(jnp.max(scores, axis=1, keepdims=True), jnp.max(draft, axis=1, keepdims=True))
        weights, draft_weights = jnp.exp2(scores - top), jnp.exp2(draft - top)
        total = jnp.sum(weights, axis=1, keepdims=True) + jnp.sum(draft_weights, axis=1, keepdims=True)
        stat_ref[i] = jnp.where(lane == 0, total, top)
        pieces.append((weights.astype(jnp.bfloat16), draft_weights.astype(jnp.bfloat16), total))
    for i, (weights, draft_weights, total) in enumerate(pieces):
        summed = jnp.dot(weights, cache_ref[1, i], preferred_element_type=jnp.float32)
        summed += jnp.dot(draft_weights, draft_ref[1, i], preferred_element_type=jnp.float32)
        out_ref[i] = (summed / total).astype(jnp.bfloat16)
        sum_ref[i] = summed


def decode(page_rows, lengths, queries, cache, draft):
    row_count, rows, _ = queries.shape
    steps, limit = draft.shape[2], cache.shape[2]
    block_rows = 8
    smem = pl.BlockSpec(memory_space=pltpu.SMEM)
    row_spec = pl.BlockSpec((block_rows, rows, HEAD), lambda r: (r, 0, 0))
    return pl.pallas_call(
        functools.partial(decode_kernel, row_count=row_count),
        grid=(row_count // block_rows,),
        out_shape=[jax.ShapeDtypeStruct(queries.shape, t) for t in (jnp.bfloat16, jnp.float32, jnp.float32)],
        in_specs=[
            smem,
            smem,
            row_spec,
            pl.BlockSpec((2, block_rows, limit, HEAD), lambda r: (0, r, 0, 0)),
            pl.BlockSpec((2, block_rows, steps, HEAD), lambda r: (0, r, 0, 0)),
        ],
        out_specs=[row_spec] * 3,
        compiler_params=pltpu.CompilerParams(vmem_limit_bytes=32 << 20),
        cost_estimate=pl.CostEstimate(flops=8 * row_count * rows * limit * HEAD, transcendentals=0, bytes_accessed=16 << 20),
        name="decode",
    )(page_rows, lengths, queries, *(pltpu.with_memory_space_constraint(x, pltpu.HBM) for x in (cache, draft)))


def page_kernel(page_rows, q_ref, out_in, sum_ref, stat_ref, far_page, near_page, out_ref):
    row_count, rows, _ = q_ref.shape
    out_ref[...] = out_in[...]
    for r, page in zip(received(page_rows, row_count), (far_page, near_page)):

        @pl.when(r >= 0)
        def _():
            scores = scores_for(q_ref[r], page[0])
            before = stat_ref[r, :, 1:2]
            top = jnp.maximum(before, jnp.max(scores, axis=1, keepdims=True))
            factor = jnp.exp2(before - top)
            weights = jnp.exp2(scores - top)
            total = stat_ref[r, :, 0:1] * factor + jnp.sum(weights, axis=1, keepdims=True)
            summed = jnp.dot(weights.astype(jnp.bfloat16), page[1], preferred_element_type=jnp.float32)
            out_ref[r] = ((sum_ref[r] * factor + summed) / total).astype(jnp.bfloat16)


def with_pages(page_rows, queries, decoded, far_page, near_page):
    return pl.pallas_call(
        page_kernel,
        out_shape=jax.ShapeDtypeStruct(queries.shape, jnp.bfloat16),
        in_specs=[pl.BlockSpec(memory_space=pltpu.SMEM)] + [pl.BlockSpec(memory_space=pltpu.VMEM)] * 6,
        compiler_params=pltpu.CompilerParams(vmem_limit_bytes=16 << 20),
        name="pages",
    )(page_rows, queries, *decoded, far_page, near_page)


def near_pages():
    return [(c, c + 1) for c in range(1, 16, 4)] + [(c, (c + 8) % 16) for c in range(3, 16, 4)]


def on_device(
    stretch_query,
    prefix_keyvals,
    stretch_key_values,
    stretch_start,
    decode_query,
    draft_key_values,
    decode_cache,
    cache_lengths,
    page_rows,
):
    row_count, steps, _ = decode_query.shape
    send = lambda x, dz, dy: lax.ppermute(x, "ctx", xor_pairs(dz, dy))
    after = lambda x, *results: lax.optimization_barrier((x, *results))[0]
    query, own, own_first, own_second = prepare(stretch_query, prefix_keyvals, stretch_key_values)
    z_first = send(own_first, 2, 0)
    keys_y = send(own, 0, 1)
    query_y = send(query, 0, 3)
    query_z = send(query, 1, 0)
    query_d = send(query, 1, 3)
    d_first = send(z_first, 0, 1)

    decode_rows = decode_query.reshape(row_count, steps * GROUP, HEAD)
    decoded = decode(page_rows, cache_lengths, decode_rows, decode_cache, draft_key_values)
    start = after(stretch_start, *decoded)
    z_second = send(after(own_second, keys_y, *decoded), 2, 0)
    d_second = send(z_second, 0, 1)
    near_source = after(stretch_key_values[0], z_first, *decoded)
    near_page = lax.ppermute(near_source, "ctx", near_pages())
    far_page = lax.ppermute(near_source, ("group", "ctx"), [(n, (n + 16) % 32) for n in range(0, 32, 2)])

    others = [query_d, query_z, query_y]
    near = whole_block(own, 0) + whole_block(keys_y, 1) + [(z_first, 0, 2, 0), (z_second, 0, 2, 1)]
    far = [(d_first, 0, 3, 0), (d_second, 0, 3, 1)]
    states = fold(start, others, 1, near, name="fold_near")
    messages = fold(start, others, 1, far, prior=states, message=True, name="fold_far")
    from_d = send(messages[0], 1, 3)
    from_z = send(messages[1], 1, 0)
    from_y = send(messages[2], 0, 3)
    start = after(start, *messages)
    (final,) = fold(start, [query], 0, near + far, name="fold_own")
    decode_rows = after(decode_rows, final)
    decode_out = with_pages(page_rows, decode_rows, decoded, far_page, near_page).reshape(decode_query.shape)
    final = after(final, decode_out)
    prefill_out = merge(final, [from_d, from_z, from_y])
    return (prefill_out, decode_out)


def solution(mesh):
    return jax.shard_map(
        on_device,
        mesh=mesh,
        in_specs=(
            P("group", "ctx", "tp"),
            P("group", None, "ctx", "tp"),
            P("group", None, "ctx", "tp"),
            P("group"),
            P(("group", "ctx"), None, "tp"),
            P(None, ("group", "ctx"), None, "tp"),
            P(None, ("group", "ctx"), None, "tp"),
            P(("group", "ctx")),
            P(),
        ),
        out_specs=(P("group", "ctx", "tp"), P(("group", "ctx"), None, "tp")),
        check_vma=False,
    )
```
